32 devices in a mesh: los: 2 (over x), sky: 16 (over z, y, core).
Axes of the slice: x: 2, y: 2, z: 4, core: 2. Of those that a mesh axis runs over, the one named last changes fastest.
Arguments:
- density: bfloat16 [16, 2048, 2048], P('los', 'sky'), may hold values from 0.1 to 10
- refine: int32 [2, 256, 256], P('los', 'sky'), may hold values from 0 to 1, as said below
- weight_low: float32 [16], P('los'), may hold values from 0.1 to 0.5
- weight_high: float32 [16], P('los'), may hold values from 0.6 to 3
Outputs:
- deflection_x: float32 [2048, 2048], P('sky', 'los')
- deflection_y: float32 [2048, 2048], P('sky', 'los')
The draws below stay inside these ranges and needn't reach their ends.
Inputs may be any that keep to these rules, and one draw needn't show every extreme that they name: `refine`: the blocks of one slab and one sky column (one index of los and of sky) hold at most 1024 refined blocks, and in every draw some slab and column holds exactly 1024.
All inputs are finite; a program needn't handle non-finite values.
Results may differ from the reference program's by a relative error of at most 0.0003.
Values may be sent and summed in bfloat16 or wider, within the bound.
A program may use at most 128 MiB of HBM per device.

```python
import math
import jax
import jax.numpy as jnp
from jax import lax

PLANE = 2048
DZ = 8
NZ = 16
CX = 128
REFINED = 1024


def draw_refine(key, part):
    slab_count = NZ // DZ
    column_count = PLANE // CX
    per_device = DZ // 8 * (CX // 8) * (PLANE // 8)
    devices = slab_count * column_count
    keys = jax.random.split(jax.random.fold_in(key, 101), devices)
    ranks = jax.vmap(lambda single: jax.random.permutation(single, per_device))(keys)
    halvings = jax.random.randint(jax.random.fold_in(key, 102), (devices,), 0, 4)
    counts = jnp.right_shift(jnp.full((devices,), REFINED, jnp.int32), halvings)
    busiest = jax.random.randint(jax.random.fold_in(key, 103), (), 0, devices)
    counts = jnp.where(jnp.arange(devices) == busiest, REFINED, counts)
    flags = (ranks < counts[:, None]).astype(jnp.int32)
    flags = flags.reshape(slab_count, column_count, DZ // 8, CX // 8, PLANE // 8)
    return flags.transpose(0, 2, 1, 3, 4).reshape(NZ // 8, PLANE // 8, PLANE // 8)


def draw_density(key, part):
    rough_span = 1.4
    ramp_span = 0.7
    noise_span = 0.15
    step_low = 0.15
    step_high = 0.35
    rough = jax.random.uniform(jax.random.fold_in(key, 211), (PLANE, PLANE), jnp.float32, -rough_span, rough_span)
    increments = jax.random.uniform(jax.random.fold_in(key, 212), (NZ,), jnp.float32, step_low, step_high)
    offset = jax.random.uniform(jax.random.fold_in(key, 213), (), jnp.float32)
    phase = offset + jnp.cumsum(increments)
    ramp = ramp_span * (2.0 * (phase - jnp.floor(phase)) - 1.0)
    noise = jax.random.uniform(jax.random.fold_in(key, 214), (NZ, PLANE, PLANE), jnp.float32, -noise_span, noise_span)
    logs = rough[None, :, :] + ramp[:, None, None] + noise
    return jnp.exp(logs).astype(jnp.bfloat16)


def block_levels(key, dims, cuts, smallest, top_value):
    loudness, own = 1.0, jax.random.fold_in(key, 6)
    for dim, parts in cuts:
        draws = jnp.exp(jax.random.uniform(jax.random.fold_in(own, dim), (parts,), jnp.float32, smallest / len(cuts), top_value / len(cuts)))
        loudness = loudness * jnp.repeat(draws, dims[dim] // parts).reshape([-1 if axis == dim else 1 for axis in range(len(dims))])
    return loudness


def setup_inputs(seed: int = 0) -> dict:
    splits = jax.random.split(jax.random.key(seed), 5)
    density = draw_density(jax.random.fold_in(splits[4], 71), 0)
    refine = draw_refine(jax.random.fold_in(splits[4], 71), 0)
    weight_low = jnp.clip(jnp.exp(math.log(0.5) - 1.609438 * jax.random.uniform(splits[2], (NZ,), jnp.float32) ** block_levels(splits[2], (NZ,), ((0, 2),), -0.2, 0.2)), 0.1, 0.5)
    weight_high = jnp.clip(jnp.exp(math.log(3.0) - 1.60943787 * jax.random.uniform(splits[3], (NZ,), jnp.float32) ** block_levels(splits[3], (NZ,), ((0, 2),), -0.2, 0.2)), 0.6, 3.0)
    return dict(density=density, refine=refine, weight_low=weight_low, weight_high=weight_high)


def minmod(former, latter):
    return 0.5 * (jnp.sign(former) + jnp.sign(latter)) * jnp.minimum(jnp.abs(former), jnp.abs(latter))


def spread(field, dimension):
    return 0.75 * field + 0.125 * (jnp.roll(field, 1, dimension) + jnp.roll(field, -1, dimension))


def slanted(field, dimension):
    return (jnp.roll(field, 1, dimension) - jnp.roll(field, -1, dimension)) / 32.0


def reference(density, refine, weight_low, weight_high):
    layers = density.shape[0]
    plane = density.shape[1]

    def layer(totals, position):
        below = lax.dynamic_index_in_dim(density, jnp.maximum(position - 1, 0), 0, keepdims=False).astype(jnp.float32)
        centre = lax.dynamic_index_in_dim(density, position, 0, keepdims=False).astype(jnp.float32)
        above = lax.dynamic_index_in_dim(density, jnp.minimum(position + 1, layers - 1), 0, keepdims=False).astype(jnp.float32)
        grad_z = minmod(above - centre, centre - below)
        grad_x = minmod(jnp.roll(centre, -1, 0) - centre, centre - jnp.roll(centre, 1, 0))
        grad_y = minmod(jnp.roll(centre, -1, 1) - centre, centre - jnp.roll(centre, 1, 1))
        coarse = lax.dynamic_index_in_dim(refine, position // 8, 0, keepdims=False).astype(jnp.float32)
        marked = jnp.repeat(jnp.repeat(coarse, 8, 0), 8, 1)
        low = lax.dynamic_index_in_dim(weight_low, position, 0, keepdims=False)
        high = lax.dynamic_index_in_dim(weight_high, position, 0, keepdims=False)
        average = 0.5 * (low + high)
        weighted = average * centre
        base, refined_base, tilt_z, tilt_x, tilt_y = totals
        return (base + weighted,
                refined_base + marked * weighted,
                tilt_z + marked * (0.125 * (high - low)) * grad_z,
                tilt_x + marked * average * grad_x,
                tilt_y + marked * average * grad_y), None

    blank = jnp.zeros((plane, plane), jnp.float32)
    totals, leftover = lax.scan(layer, (blank, blank, blank, blank, blank), jnp.arange(layers, dtype=jnp.int32))
    base, refined_base, tilt_z, tilt_x, tilt_y = totals
    smoothed = spread(refined_base + tilt_z, 1) + slanted(tilt_y, 1)
    kappa = (base - refined_base + spread(smoothed, 0) + slanted(spread(tilt_x, 1), 0)) / jnp.float32(layers)
    spectrum = jnp.fft.fft2(kappa)
    wave = 2.0 * jnp.pi * jnp.fft.fftfreq(plane)
    wave_x = wave[:, None]
    wave_y = wave[None, :]
    squared = wave_x * wave_x + wave_y * wave_y
    at_anchor = squared == 0
    potential = jnp.where(at_anchor, 0.0, -2.0 / jnp.where(at_anchor, 1.0, squared)) * spectrum
    deflection_x = jnp.real(jnp.fft.ifft2(1j * wave_x * potential)).astype(jnp.float32)
    deflection_y = jnp.real(jnp.fft.ifft2(1j * wave_y * potential)).astype(jnp.float32)
    return (deflection_x, deflection_y)
```

```python
import functools
import math

import jax
import jax.numpy as jnp
import numpy as np
from jax import lax
from jax.experimental import pallas as pl
from jax.experimental.pallas import tpu as pltpu
from jax.sharding import PartitionSpec as P

LANES = 128
SUB = 8
VMEM = pl.BlockSpec(memory_space=pltpu.VMEM)
SMEM = pl.BlockSpec(memory_space=pltpu.SMEM)


def median0(a, b):
    return jnp.maximum(jnp.minimum(a, b), jnp.minimum(jnp.maximum(a, b), 0.0))


def add(p, q):
    im = q[1] if p[1] is None else (p[1] if q[1] is None else p[1] + q[1])
    return (p[0] + q[0], im)


def sub(p, q):
    if q[1] is None:
        return (p[0] - q[0], p[1])
    return (p[0] - q[0], -q[1] if p[1] is None else p[1] - q[1])


def turn(p, angle):
    c, s = math.cos(angle), math.sin(angle)
    re, im = p
    if abs(s) < 1e-12:
        return p if c > 0 else (-re, None if im is None else -im)
    if abs(c) < 1e-12:
        sign = 1.0 if s > 0 else -1.0
        if im is None:
            return (jnp.zeros_like(re), sign * re)
        return (-im, re) if s > 0 else (im, -re)
    if im is None:
        return (c * re, s * re)
    return (c * re - s * im, s * re + c * im)


def fft_list(items, flip):
    count = len(items)
    if count == 1:
        return items
    even = fft_list(items[0::2], flip)
    odd = fft_list(items[1::2], flip)
    first, second = [], []
    for k in range(count // 2):
        w = turn(odd[k], flip * 2.0 * math.pi * k / count)
        first.append(add(even[k], w))
        second.append(sub(even[k], w))
    return first + second


def row_table(width):
    tiles = width // LANES
    classes = tiles // 2
    half = LANES // 2
    t = np.arange(LANES)
    table = np.zeros((classes, 2 * LANES, 2 * LANES))

    def angles(n):
        return 2.0 * np.pi * ((n[:, None] * t[None, :]) % width) / width

    for c in range(classes):
        if c == 0:
            j = np.arange(half)
            low = angles(tiles * j)
            high = angles(tiles * j + classes)
            table[0, :half, :LANES] = np.cos(low)
            table[0, half:LANES, LANES:] = np.cos(high)
            table[0, LANES : LANES + half, :LANES] = -np.sin(low)
            table[0, LANES, :LANES] = np.cos(np.pi * t)
            table[0, LANES + half :, LANES:] = -np.sin(high)
        else:
            a = angles(c + tiles * np.arange(LANES))
            table[c, :LANES, :LANES] = np.cos(a)
            table[c, :LANES, LANES:] = np.sin(a)
            table[c, LANES:, :LANES] = -np.sin(a)
            table[c, LANES:, LANES:] = np.cos(a)
    return jnp.asarray(table, jnp.float32)


def tile_table(width):
    tiles = width // LANES
    classes = tiles // 2
    s = np.arange(tiles)
    table = np.zeros((classes, 2 * tiles))
    for c in range(classes):
        if c == 0:
            table[c, 0::2] = 1.0
            table[c, 1::2] = np.where(s % 2 == 0, 1.0, -1.0)
        else:
            table[c, 0::2] = np.cos(2.0 * np.pi * s * c / tiles)
            table[c, 1::2] = -np.sin(2.0 * np.pi * s * c / tiles)
    return jnp.asarray(table, jnp.float32)


def column_tables(length, sky):
    rows = length // sky
    t = np.arange(rows)
    a = 2.0 * np.pi * (t[:, None] * t[None, :] % rows) / rows
    c, s = np.cos(a), np.sin(a)
    forward = np.block([[c, -s], [s, c]])
    b = 2.0 * np.pi * (np.arange(sky)[:, None] * t[None, :]) / length
    twist = np.stack([np.cos(b), np.sin(b)], axis=1)
    return jnp.asarray(forward, jnp.float32), jnp.asarray(twist, jnp.float32)


def dot(a, b, dims):
    return lax.dot_general(
        a, b, (dims, ((), ())), precision=lax.Precision.HIGHEST, preferred_element_type=jnp.float32
    )


def sums_kernel(
    average, slope, density, first, final, out, below, above, before, after, cells, send, receive
):
    layers, rows, width = density.shape
    los, sky = lax.axis_index("los"), lax.axis_index("sky")
    los_count, sky_count = lax.axis_size("los"), lax.axis_size("sky")
    barrier = pltpu.get_barrier_semaphore()
    mesh = pl.DeviceIdType.MESH
    for axis, me, count in (("los", los, los_count), ("sky", sky, sky_count)):
        for shift in (1, count - 1):
            pl.semaphore_signal(barrier, inc=1, device_id={axis: lax.rem(me + shift, count)}, device_id_type=mesh)
    pl.semaphore_wait(barrier, 4)

    def hop(source, target, i, axis, me, count, shift):
        return pltpu.make_async_remote_copy(
            src_ref=source,
            dst_ref=target,
            send_sem=send.at[i],
            recv_sem=receive.at[i],
            device_id={axis: lax.rem(me + shift, count)},
            device_id_type=mesh,
        )

    onward = hop(density.at[layers - 1], below, 0, "los", los, los_count, 1)
    back = hop(density.at[0], above, 1, "los", los, los_count, los_count - 1)
    forth = hop(final, before, 2, "sky", sky, sky_count, 1)
    prior = hop(first, after, 3, "sky", sky, sky_count, sky_count - 1)
    has_next, has_prior = los < los_count - 1, los > 0
    pl.when(has_next)(onward.start)
    pl.when(has_prior)(back.start)
    forth.start()
    prior.start()
    deep = 16
    last = density[:, rows - deep : rows, :]
    head = density[:, 0:deep, :]
    for z in range(layers):
        cells[z, SUB - 1 : SUB, :] = head[z].astype(jnp.float32)[0:1]
        cells[z, SUB + rows : SUB + rows + 1, :] = last[z].astype(jnp.float32)[deep - 1 : deep]

    def fill(r, carry):
        start = pl.multiple_of(r * deep, deep)
        into = pl.ds(pl.multiple_of(start + SUB, SUB), deep)
        for z in range(layers):
            cells[z, into, :] = density[z, pl.ds(start, deep), :].astype(jnp.float32)
        return carry

    lax.fori_loop(0, rows // deep, fill, 0)

    def chunk(r, carry):
        start = pl.multiple_of(r * SUB, SUB)
        here = pl.ds(pl.multiple_of(start + SUB, SUB), SUB)
        mid = cells[0, here, :]
        step_z = None
        base = jnp.zeros((SUB, width), jnp.float32)
        tilt_z, tilt_x, tilt_y = base, base, base
        for z in range(layers):
            w = cells[z, pl.ds(start, 3 * SUB), :]
            up, down = w[SUB - 1 : 2 * SUB - 1], w[SUB + 1 : 2 * SUB + 1]
            step_y = pltpu.roll(mid, width - 1, 1) - mid
            back_y = pltpu.roll(step_y, 1, 1)
            base = base + average[z] * mid
            tilt_x = tilt_x + average[z] * median0(down - mid, mid - up)
            tilt_y = tilt_y + average[z] * median0(step_y, back_y)
            if z < layers - 1:
                above = cells[z + 1, here, :]
                next_z = above - mid
                if z > 0:
                    tilt_z = tilt_z + slope[z] * median0(next_z, step_z)
                mid, step_z = above, next_z
        rows_at = pl.ds(start, SUB)
        out[0, rows_at, :] = base
        out[1, rows_at, :] = tilt_z
        out[2, rows_at, :] = tilt_x
        out[3, rows_at, :] = tilt_y
        return carry

    lax.fori_loop(0, rows // SUB, chunk, 0)
    forth.wait()
    prior.wait()
    pl.when(has_next)(onward.wait_send)
    pl.when(has_prior)(onward.wait_recv)
    pl.when(has_prior)(back.wait_send)
    pl.when(has_next)(back.wait_recv)


def edge_kernel(
    sums, low, high, below, above, before, first, second, former, final, after, refine, column_average, slope, keep,
    place, out, rims, base_s, smooth_s, tilt_s
):
    rows, width = below.shape
    tiles = width // LANES
    los_count, groups = out.shape[0], out.shape[1]
    blocks, coarse = refine.shape
    deep = 16
    weight = column_average[...]

    def rim_slope(one, two, three):
        one, two, three = [ref[...].astype(jnp.float32) for ref in (one, two, three)]
        return jnp.sum(weight * median0(three - two, two - one), axis=0, keepdims=True)

    fix_first = rim_slope(before, first, second)
    fix_last = rim_slope(former, final, after)
    blank = jnp.zeros((2 * SUB, width), jnp.float32)
    for ref in (smooth_s, tilt_s):
        ref[0 : 2 * SUB, :] = blank
        ref[rows + 2 * SUB : rows + 4 * SUB, :] = blank
    base_s[0:SUB, :] = blank[:SUB]
    base_s[rows + SUB : rows + 2 * SUB, :] = blank[:SUB]
    column = lax.broadcasted_iota(jnp.int32, (coarse, width), 1)
    line = lax.broadcasted_iota(jnp.int32, (coarse, width), 0)
    wide = width // coarse
    inside = (column >= line * wide) & (column < line * wide + wide)
    stretch = jnp.where(inside, 1.0, 0.0).astype(jnp.bfloat16)
    marks = jnp.dot(
        refine[...].astype(jnp.float32).astype(jnp.bfloat16), stretch, preferred_element_type=jnp.float32
    )
    for r in range(blocks):
        base_s[SUB * (r + 1) : SUB * (r + 2), :] = jnp.broadcast_to(marks[r : r + 1], (SUB, width))

    def spread(field):
        return 0.75 * field + 0.125 * (pltpu.roll(field, 1, 1) + pltpu.roll(field, width - 1, 1))

    end = low.shape[0]

    def chunk(r, carry):
        start = pl.multiple_of(r * deep, deep)
        here = pl.ds(start, deep)
        base, tilt_z, tilt_x, tilt_y = [sums[i, here, :] for i in range(4)]
        v0, v1 = [low[i, here, :].astype(jnp.float32) for i in range(2)]
        v6, v7 = [high[i, here, :].astype(jnp.float32) for i in range(2)]
        under, over = below[here, :].astype(jnp.float32), above[here, :].astype(jnp.float32)
        tilt_z = tilt_z + slope[0] * median0(v1 - v0, jnp.where(keep[0] > 0.0, v0 - under, 0.0))
        tilt_z = tilt_z + slope[slope.shape[0] - 1] * median0(jnp.where(keep[1] > 0.0, over - v7, 0.0), v7 - v6)
        at = lax.broadcasted_iota(jnp.int32, (deep, width), 0) + start
        tilt_x = tilt_x + jnp.where(at == 0, fix_first, 0.0) + jnp.where(at == rows - 1, fix_last, 0.0)
        ours = pl.ds(pl.multiple_of(start + SUB, SUB), deep)
        mark = base_s[ours, :]
        refined = mark * base
        base_s[ours, :] = base - refined
        tilt_y = mark * tilt_y
        into = pl.ds(pl.multiple_of(start + 2 * SUB, SUB), deep)
        smooth_s[into, :] = spread(refined + mark * tilt_z) + (
            pltpu.roll(tilt_y, 1, 1) - pltpu.roll(tilt_y, width - 1, 1)
        ) * (1.0 / 32.0)
        tilt_s[into, :] = spread(mark * tilt_x)
        return carry

    lax.fori_loop(0, rows // deep, chunk, 0)

    def pairs(start):
        a = smooth_s[pl.ds(start, 3 * SUB), :]
        b = tilt_s[pl.ds(start, 3 * SUB), :]
        prior, mid, later = slice(SUB - 1, 2 * SUB - 1), slice(SUB, 2 * SUB), slice(SUB + 1, 2 * SUB + 1)
        deposit = (
            base_s[pl.ds(start, SUB), :]
            + 0.75 * a[mid]
            + 0.125 * (a[prior] + a[later])
            + (b[prior] - b[later]) * (1.0 / 32.0)
        )
        parts = [(deposit[:, LANES * s : LANES * (s + 1)], None) for s in range(tiles)]
        modes = fft_list(parts, -1.0)
        return [(modes[0][0], modes[tiles // 2][0])] + modes[1 : tiles // 2]

    def finish(r, carry):
        into = pl.ds(pl.multiple_of(r * SUB, SUB), SUB)
        for c, pair in enumerate(pairs(pl.multiple_of((r + 1) * SUB, SUB))):
            relative = lax.rem(c // groups - place[0] + los_count, los_count)
            for j in range(2):
                out[relative, c % groups, j, into, :] = pair[j]
        return carry

    lax.fori_loop(0, rows // SUB, finish, 0)
    for edge, (start, row) in enumerate(((0, SUB - 1), (rows + SUB, 0))):
        for c, pair in enumerate(pairs(start)):
            for j in range(2):
                rims[edge, c, j : j + 1, :] = pair[j][row : row + 1]


def pack(re, im, spare=None):
    size = jnp.max(jnp.maximum(jnp.abs(re), jnp.abs(im)), axis=0, keepdims=True)
    if spare is not None:
        size = jnp.maximum(size, jnp.abs(spare) * (1.0 / 16384.0))
    level = jnp.ceil(jnp.log2(jnp.maximum(size, 1e-30) * (1.0 / 32700.0)) * 32.0)
    inverse = jnp.exp2(level * (-1.0 / 32.0))
    high = (re * inverse + 32768.5).astype(jnp.int32)
    low = (im * inverse + 32768.5).astype(jnp.int32)
    words = lax.shift_left(high, jnp.full_like(high, 16)) | low
    wide = None if spare is None else (spare * inverse).astype(jnp.int32)
    return words, level.astype(jnp.int32), wide


def unpack(words, level):
    step = jnp.exp2(level.astype(jnp.float32) * (1.0 / 32.0))
    high = lax.shift_right_logical(words, jnp.full_like(words, 16)).astype(jnp.float32)
    low = (words & 65535).astype(jnp.float32)
    return (high - 32768.0) * step, (low - 32768.0) * step, step


def spectral_kernel(length, layers, los_count, sky_count, groups, chunks, *refs):
    folded = refs[:los_count]
    (
        rims, table_in, forward, twist, mix, out_x, out_y,
        table, spectra, fsend, frecv, bsend, brecv, cross, scales, local,
        fs, fr, bs, br, xs, xr,
    ) = refs[los_count:]
    outs = (out_x, out_y)
    mesh = pl.DeviceIdType.MESH
    los, sky = lax.axis_index("los"), lax.axis_index("sky")
    barrier = pltpu.get_barrier_semaphore()
    for i in range(1, sky_count):
        pl.semaphore_signal(barrier, inc=1, device_id={"sky": lax.rem(sky + i, sky_count)}, device_id_type=mesh)
    for i in range(1, los_count):
        pl.semaphore_signal(barrier, inc=1, device_id={"los": lax.rem(los + i, los_count)}, device_id_type=mesh)
    fetch = pltpu.make_async_copy(table_in, table, local)
    fetch.start()
    _, pair, rows, _ = folded[0].shape
    part = LANES // sky_count
    each = groups // chunks
    count = each * part
    classes = length // LANES // 2
    tiles = 2 * classes
    half = LANES // 2

    def mode_of(kind, j):
        n = jnp.where(kind == 0, jnp.where(j < half, tiles * j, tiles * (j - half) + classes), kind + tiles * j)
        return jnp.where(n >= length // 2, n - length, n)

    def sky_copy(source, target, send, recv, i):
        peer = lax.rem(sky + i, sky_count)
        return pltpu.make_async_remote_copy(
            src_ref=source(peer), dst_ref=target, send_sem=send, recv_sem=recv,
            device_id={"sky": peer}, device_id_type=mesh,
        )

    def forward_copy(c, i):
        size = count + (2 if c == 0 else 1)
        return sky_copy(
            lambda peer: fsend.at[c, peer, pl.ds(0, size)], frecv.at[c, sky, pl.ds(0, size)],
            fs.at[c, i], fr.at[c, i], i,
        )

    def backward_copy(f, c, i):
        return sky_copy(
            lambda peer: bsend.at[f, c, peer, pl.ds(0, count + 1)], brecv.at[f, c, sky, pl.ds(0, count + 1)],
            bs.at[f, c, i], br.at[f, c, i], i,
        )

    def cross_copy(f, c, i):
        return pltpu.make_async_remote_copy(
            src_ref=brecv.at[f, c, :, pl.ds(0, count + 1)],
            dst_ref=cross.at[los_count - 1 - i, f, c, :, pl.ds(0, count + 1)],
            send_sem=xs.at[f, c, i], recv_sem=xr.at[f, c, i],
            device_id={"los": lax.rem(los + i, los_count)}, device_id_type=mesh,
        )

    line = lax.broadcasted_iota(jnp.int32, (rows, LANES), 0)
    order = lax.broadcasted_iota(jnp.int32, (LANES, rows), 0)
    fetch.wait()
    for c in range(chunks):
        for g in range(c * each, (c + 1) * each):
            sides = []
            for j in range(pair):
                side = folded[0][g, j]
                for other in folded[1:]:
                    side = side + other[g, j]
                side = side + jnp.where(line == 0, rims[0, g, j : j + 1, :], 0.0)
                side = side + jnp.where(line == rows - 1, rims[1, g, j : j + 1, :], 0.0)
                sides.append(side)
            kind = los * groups + g
            z = dot(table[kind], jnp.concatenate(sides, axis=1), ((1,), (1,)))
            n = jnp.maximum(jnp.abs(mode_of(kind, order)), 1).astype(jnp.float32)
            weight = lax.rsqrt(n)
            nyquist = (kind == 0) & (order == 0)
            spectra[g, 0] = z[:LANES] * weight
            spectra[g, 1] = z[LANES:] * jnp.where(nyquist, 1.0 / math.sqrt(length // 2), weight)
        for d in range(sky_count):
            re, im = [
                jnp.concatenate(
                    [spectra[g, j, d * part : (d + 1) * part, :] for g in range(c * each, (c + 1) * each)], axis=0
                )
                for j in range(pair)
            ]
            spare = None
            if c == 0:
                spare = re[0:1]
                re = jnp.where(lax.broadcasted_iota(jnp.int32, re.shape, 0) == 0, 0.0, re)
            words, level, wide = pack(re, im, spare)
            fsend[c, d, 0:count, :] = words
            fsend[c, d, count : count + 1, :] = level
            if c == 0:
                fsend[c, d, count + 1 : count + 2, :] = wide
        if c == 0:
            pl.semaphore_wait(barrier, sky_count + los_count - 2)
        for i in range(1, sky_count):
            forward_copy(c, i).start()
        frecv[c, pl.ds(sky, 1)] = fsend[c, pl.ds(sky, 1)]

    unit = 2.0 * math.pi / length
    base = -2.0 / (unit * float(length) * float(length) * float(layers))

    def masks(c, shape):
        line = lax.broadcasted_iota(jnp.int32, shape, 0)
        packed = (line == 0) & (los == 0) & (sky == 0) if c == 0 else None
        return line, packed

    for c in range(chunks):
        extra = SUB if c == 0 else 0
        total = count + extra
        line, packed = masks(c, (total, rows))
        lane = lax.broadcasted_iota(jnp.int32, (total, rows), 1)
        n = mode_of(los * groups + c * each + line // part, sky * part + line % part)
        single = line >= count
        if c == 0:
            n = jnp.where(single, length // 2, n)
            single = single | packed
        ny = n.astype(jnp.float32)
        odd_y = jnp.where(n == length // 2, 0.0, ny)
        weight = jnp.where(single, base, 2.0 * base) * jnp.sqrt(jnp.maximum(jnp.abs(ny), 1.0))
        for k in range(sky_count):
            nx = k + sky_count * lane
            nx = jnp.where(nx >= length // 2, nx - length, nx)
            odd_x = jnp.where(nx == -(length // 2), 0, nx).astype(jnp.float32)
            square = nx.astype(jnp.float32) * nx.astype(jnp.float32) + ny * ny
            factor = jnp.where(square == 0.0, 0.0, weight / jnp.where(square == 0.0, 1.0, square))
            scales[c, 0, k, 0:total, :] = odd_x * factor
            scales[c, 1, k, 0:total, :] = odd_y * factor

    for c in range(chunks):
        extra = SUB if c == 0 else 0
        total = count + extra
        line, packed = masks(c, (total, rows))
        for i in range(1, sky_count):
            forward_copy(c, i).wait_recv()
        items = []
        for s in range(sky_count):
            re, im, step = unpack(frecv[c, s, 0:count, :], frecv[c, s, count : count + 1, :])
            if c == 0:
                wide = frecv[c, s, count + 1 : count + 2, :].astype(jnp.float32) * step
                re = jnp.where(line[:count] == 0, wide, re)
                zero = jnp.zeros((extra, rows), jnp.float32)
                re = jnp.concatenate([re, jnp.broadcast_to(im[0:1], (extra, rows))], axis=0)
                im = jnp.where(packed, 0.0, jnp.concatenate([im, zero], axis=0))
            items.append((re, im))
        items = fft_list(items, -1.0)
        turned = []
        for k, (re, im) in enumerate(items):
            co, si = twist[k, 0:1, :], twist[k, 1:2, :]
            turned.append(jnp.concatenate([re * co + im * si, im * co - re * si], axis=1))
        spectrum = dot(jnp.concatenate(turned, axis=0), forward[...], ((1,), (0,)))
        for f in range(2):
            fields = []
            for k in range(sky_count):
                here = spectrum[k * total : (k + 1) * total]
                scale = scales[c, f, k, 0:total, :]
                fields.append(jnp.concatenate([-scale * here[:, rows:], scale * here[:, :rows]], axis=1))
            values = dot(jnp.concatenate(fields, axis=0), forward[...], ((1,), (1,)))
            items = []
            for k in range(sky_count):
                here = values[k * total : (k + 1) * total]
                re, im = here[:, :rows], here[:, rows:]
                co, si = twist[k, 0:1, :], twist[k, 1:2, :]
                items.append((re * co - im * si, im * co + re * si))
            items = fft_list(items, 1.0)
            for s in range(sky_count):
                re, im = items[s]
                if c == 0:
                    im = jnp.where(packed[:count], jnp.broadcast_to(re[count : count + 1], (count, rows)), im[:count])
                    re = re[:count]
                words, level, _ = pack(re, im)
                bsend[f, c, s, 0:count, :] = words
                bsend[f, c, s, count : count + 1, :] = level
            for i in range(1, sky_count):
                backward_copy(f, c, i).start()
            brecv[f, c, pl.ds(sky, 1)] = bsend[f, c, pl.ds(sky, 1)]

    inner = out_x.shape[1] // LANES
    fresh = [True, True]

    def plane(f, c, block, owner):
        parts = [unpack(block[s, 0:count, :], block[s, count : count + 1, :]) for s in range(sky_count)]
        pieces = []
        for g in range(each):
            z = jnp.concatenate([p[j][g * part : (g + 1) * part] for j in range(pair) for p in parts], axis=0)
            kind = owner * groups + c * each + g
            both = dot(z, table[kind], ((0,), (0,)))
            pieces.append((kind, both[:, :LANES], both[:, LANES:]))
        for i in range(inner):
            at = 2 * (los * inner + i)
            tile = slice(i * LANES, (i + 1) * LANES)
            total = None if fresh[f] else outs[f][:, tile]
            for kind, one, two in pieces:
                term = mix[kind, at] * one + mix[kind, at + 1] * two
                total = term if total is None else total + term
            outs[f][:, tile] = total
        fresh[f] = False

    def arrive(f, c):
        for i in range(1, sky_count):
            backward_copy(f, c, i).wait_recv()
        for i in range(1, los_count):
            cross_copy(f, c, i).start()
        plane(f, c, brecv.at[f, c], los)

    def collect(f, c):
        for i in range(1, los_count):
            cross_copy(f, c, i).wait_recv()
            slot = los_count - 1 - i
            plane(f, c, cross.at[slot, f, c], lax.rem(los + los_count - i, los_count))

    steps = [(f, c) for c in range(chunks) for f in range(2)]
    for at, step in enumerate(steps):
        arrive(*step)
        if at:
            collect(*steps[at - 1])
    collect(*steps[-1])
    for c in range(chunks):
        for i in range(1, sky_count):
            forward_copy(c, i).wait_send()
            for f in range(2):
                backward_copy(f, c, i).wait_send()
        for f in range(2):
            for i in range(1, los_count):
                cross_copy(f, c, i).wait_send()


def call(kernel, shapes, specs, scratch=(), work=1, grid=(), types=jnp.float32, number=None):
    if not isinstance(types, tuple):
        types = jax.tree.map(lambda shape: types, shapes, is_leaf=lambda s: isinstance(s[0], int))
    return pl.pallas_call(
        kernel,
        grid=grid,
        out_shape=jax.tree.map(
            jax.ShapeDtypeStruct, shapes, types, is_leaf=lambda s: isinstance(s[0], int)
        ),
        in_specs=specs,
        out_specs=jax.tree.map(lambda shape: VMEM, shapes, is_leaf=lambda s: isinstance(s[0], int)),
        scratch_shapes=list(scratch),
        cost_estimate=pl.CostEstimate(flops=work, bytes_accessed=work, transcendentals=0),
        compiler_params=pltpu.CompilerParams(
            vmem_limit_bytes=60 * 1024 * 1024, collective_id=number, has_side_effects=number is not None
        ),
    )


def body(density, refine, weight_low, weight_high):
    los_count = lax.axis_size("los")
    sky_count = lax.axis_size("sky")
    los = lax.axis_index("los")
    sky = lax.axis_index("sky")
    layers, rows, width = density.shape
    length = rows * sky_count
    tiles = width // LANES
    classes = tiles // 2
    groups = classes // los_count
    part = LANES // sky_count
    place = jnp.stack([los, sky]).astype(jnp.int32)
    ring = [(i, (i + 1) % sky_count) for i in range(sky_count)]
    gnir = [((i + 1) % sky_count, i) for i in range(sky_count)]

    def to_shift(values, shift):
        return lax.ppermute(values, "los", [(i, (i + shift) % los_count) for i in range(los_count)])

    first, second = density[:, 0, :], density[:, 1, :]
    former, final = density[:, rows - 2, :], density[:, rows - 1, :]
    average = 0.5 * (weight_low + weight_high)
    slope = 0.125 * (weight_high - weight_low)
    keep = jnp.stack([los > 0, los < los_count - 1]).astype(jnp.float32)
    half = jnp.bfloat16
    sums, below, above, before, after = call(
        sums_kernel,
        ((4, rows, width), (rows, width), (rows, width), (layers, width), (layers, width)),
        [SMEM, SMEM] + [VMEM] * 3,
        [
            pltpu.VMEM((layers, rows + 2 * SUB, width), jnp.float32),
            pltpu.SemaphoreType.DMA((4,)),
            pltpu.SemaphoreType.DMA((4,)),
        ],
        work=40_000_000,
        types=(jnp.float32, half, half, half, half),
        number=3,
    )(average, slope, density, first, final)
    two = (2, rows, width)
    folded, rims = call(
        edge_kernel,
        ((los_count, groups, 2, rows, LANES), (2, classes, 2, LANES)),
        [
            VMEM,
            pl.BlockSpec(two, lambda i: (0, 0, 0), memory_space=pltpu.VMEM),
            pl.BlockSpec(two, lambda i: (layers // 2 - 1, 0, 0), memory_space=pltpu.VMEM),
        ]
        + [VMEM] * 10
        + [SMEM] * 3,
        [
            pltpu.VMEM((rows + 2 * SUB, width), jnp.float32),
            pltpu.VMEM((rows + 4 * SUB, width), jnp.float32),
            pltpu.VMEM((rows + 4 * SUB, width), jnp.float32),
        ],
        grid=(1,),
    )(
        sums, density, density, below, above, before, first, second, former, final, after, refine[0],
        average[:, None], slope, keep, place,
    )
    others = [to_shift(folded[shift], shift) for shift in range(1, los_count)]
    from_before = lax.ppermute(rims[1], "sky", ring)
    from_after = lax.ppermute(rims[0], "sky", gnir)
    rims = jnp.stack([from_before, from_after])

    def rims_of(shift):
        return lax.dynamic_slice_in_dim(rims, (los + shift) % los_count * groups, groups, 1)

    gathered = rims_of(0)
    for shift in range(1, los_count):
        gathered = gathered + to_shift(rims_of(shift), shift)
    table = row_table(width)
    forward, twist = column_tables(length, sky_count)
    mix = tile_table(width)
    out_width = width // los_count
    chunks = 2 if groups % 2 == 0 else 1
    deep = groups // chunks * part + SUB
    peers = (sky_count, -(-deep // SUB) * SUB, rows)
    dma = pltpu.SemaphoreType.DMA
    return pl.pallas_call(
        functools.partial(
            spectral_kernel, length, layers * los_count, los_count, sky_count, groups, chunks
        ),
        out_shape=(jax.ShapeDtypeStruct((rows, out_width), jnp.float32),) * 2,
        in_specs=[VMEM] * (los_count + 1) + [pl.BlockSpec(memory_space=pl.ANY), VMEM, VMEM, SMEM],
        out_specs=(VMEM, VMEM),
        scratch_shapes=[
            pltpu.VMEM(table.shape, jnp.float32),
            pltpu.VMEM((groups, 2, LANES, rows), jnp.float32),
            pltpu.VMEM((chunks,) + peers, jnp.int32),
            pltpu.VMEM((chunks,) + peers, jnp.int32),
            pltpu.VMEM((2, chunks) + peers, jnp.int32),
            pltpu.VMEM((2, chunks) + peers, jnp.int32),
            pltpu.VMEM((los_count - 1, 2, chunks) + peers, jnp.int32),
            pltpu.VMEM((chunks, 2) + peers, jnp.float32),
            dma,
            dma((chunks, sky_count)),
            dma((chunks, sky_count)),
            dma((2, chunks, sky_count)),
            dma((2, chunks, sky_count)),
            dma((2, chunks, los_count)),
            dma((2, chunks, los_count)),
        ],
        compiler_params=pltpu.CompilerParams(
            vmem_limit_bytes=48 * 1024 * 1024, collective_id=0, has_side_effects=True
        ),
    )(folded[0], *others, gathered, table, forward, twist, mix)


def solution(mesh):
    placed = (P("los", "sky", None), P("los", "sky", None), P("los"), P("los"))
    return jax.shard_map(
        body,
        mesh=mesh,
        in_specs=placed,
        out_specs=(P("sky", "los"), P("sky", "los")),
        check_vma=False,
    )
```

```python
import functools
import math

import jax
import jax.numpy as jnp
import numpy as np
from jax import lax
from jax.experimental import pallas as pl
from jax.experimental.pallas import tpu as pltpu
from jax.sharding import PartitionSpec as P

LANES = 128
SUB = 8
VMEM = pl.BlockSpec(memory_space=pltpu.VMEM)
SMEM = pl.BlockSpec(memory_space=pltpu.SMEM)
ANY = pl.BlockSpec(memory_space=pl.ANY)


def median0(a, b):
    return jnp.maximum(jnp.minimum(a, b), jnp.minimum(jnp.maximum(a, b), 0.0))


def add(p, q):
    im = q[1] if p[1] is None else (p[1] if q[1] is None else p[1] + q[1])
    return (p[0] + q[0], im)


def sub(p, q):
    if q[1] is None:
        return (p[0] - q[0], p[1])
    return (p[0] - q[0], -q[1] if p[1] is None else p[1] - q[1])


def turn(p, angle):
    c, s = math.cos(angle), math.sin(angle)
    re, im = p
    if abs(s) < 1e-12:
        return p if c > 0 else (-re, None if im is None else -im)
    if abs(c) < 1e-12:
        sign = 1.0 if s > 0 else -1.0
        if im is None:
            return (jnp.zeros_like(re), sign * re)
        return (-im, re) if s > 0 else (im, -re)
    if im is None:
        return (c * re, s * re)
    return (c * re - s * im, s * re + c * im)


def fft_list(items, flip):
    count = len(items)
    if count == 1:
        return items
    even = fft_list(items[0::2], flip)
    odd = fft_list(items[1::2], flip)
    first, second = [], []
    for k in range(count // 2):
        w = turn(odd[k], flip * 2.0 * math.pi * k / count)
        first.append(add(even[k], w))
        second.append(sub(even[k], w))
    return first + second


def row_table(width):
    tiles = width // LANES
    classes = tiles // 2
    half = LANES // 2
    t = np.arange(LANES)
    table = np.zeros((classes, 2 * LANES, 2 * LANES))

    def angles(n):
        return 2.0 * np.pi * ((n[:, None] * t[None, :]) % width) / width

    for c in range(classes):
        if c == 0:
            j = np.arange(half)
            low = angles(tiles * j)
            high = angles(tiles * j + classes)
            table[0, :half, :LANES] = np.cos(low)
            table[0, half:LANES, LANES:] = np.cos(high)
            table[0, LANES : LANES + half, :LANES] = -np.sin(low)
            table[0, LANES, :LANES] = np.cos(np.pi * t)
            table[0, LANES + half :, LANES:] = -np.sin(high)
        else:
            a = angles(c + tiles * np.arange(LANES))
            table[c, :LANES, :LANES] = np.cos(a)
            table[c, :LANES, LANES:] = np.sin(a)
            table[c, LANES:, :LANES] = -np.sin(a)
            table[c, LANES:, LANES:] = np.cos(a)
    return jnp.asarray(table, jnp.float32)


def tile_table(width):
    tiles = width // LANES
    classes = tiles // 2
    s = np.arange(tiles)
    table = np.zeros((classes, 2 * tiles))
    for c in range(classes):
        if c == 0:
            table[c, 0::2] = 1.0
            table[c, 1::2] = np.where(s % 2 == 0, 1.0, -1.0)
        else:
            table[c, 0::2] = np.cos(2.0 * np.pi * s * c / tiles)
            table[c, 1::2] = -np.sin(2.0 * np.pi * s * c / tiles)
    return jnp.asarray(table, jnp.float32)


def column_tables(length, sky):
    rows = length // sky
    t = np.arange(rows)
    a = 2.0 * np.pi * (t[:, None] * t[None, :] % rows) / rows
    c, s = np.cos(a), np.sin(a)
    forward = np.block([[c, -s], [s, c]])
    b = 2.0 * np.pi * (np.arange(sky)[:, None] * t[None, :]) / length
    twist = np.stack([np.cos(b), np.sin(b)], axis=1)
    return jnp.asarray(forward, jnp.float32), jnp.asarray(twist, jnp.float32)


def dot(a, b, dims):
    return lax.dot_general(
        a, b, (dims, ((), ())), precision=lax.Precision.HIGHEST, preferred_element_type=jnp.float32
    )


def pack(re, im, spare=None, centred=False):
    size = jnp.max(jnp.maximum(jnp.abs(re - spare if centred else re), jnp.abs(im)), axis=0, keepdims=True)
    if spare is not None:
        size = jnp.maximum(size, jnp.abs(spare) * (1.0 / 16384.0))
    level = jnp.ceil(jnp.log2(jnp.maximum(size, 1e-30) * (1.0 / 32700.0)) * 32.0)
    inverse = jnp.exp2(level * (-1.0 / 32.0))
    wide = None if spare is None else jnp.floor(spare * inverse + 0.5).astype(jnp.int32)
    if centred:
        re = re - wide.astype(jnp.float32) * jnp.exp2(level * (1.0 / 32.0))
    high = (re * inverse + 32768.5).astype(jnp.int32)
    low = (im * inverse + 32768.5).astype(jnp.int32)
    words = lax.shift_left(high, jnp.full_like(high, 16)) | low
    return words, level.astype(jnp.int32), wide


def unpack(words, level):
    step = jnp.exp2(level.astype(jnp.float32) * (1.0 / 32.0))
    high = lax.shift_right_logical(words, jnp.full_like(words, 16)).astype(jnp.float32)
    low = (words & 65535).astype(jnp.float32)
    return (high - 32768.0) * step, (low - 32768.0) * step, step


def lens_kernel(length, los_count, sky_count, groups, chunks, *refs):
    (
        density, refine_in, weight_low, weight_high, table_in, forward_in, twist_in, mix, out_x, out_y,
        raw, cells, below, above, marks, sums, rest, smooth, tilt, fold, hop_send, hop_recv,
        table, forward, twist, refine, spectra, fsend, frecv, bsend, brecv, cross, scales, local,
        loads, halo_s, halo_r, hs, hr, fs, fr, bs, br, xs, xr,
    ) = refs
    outs = (out_x, out_y)
    mesh = pl.DeviceIdType.MESH
    los, sky = lax.axis_index("los"), lax.axis_index("sky")
    barrier = pltpu.get_barrier_semaphore()
    for i in range(1, sky_count):
        pl.semaphore_signal(barrier, inc=1, device_id={"sky": lax.rem(sky + i, sky_count)}, device_id_type=mesh)
    for i in range(1, los_count):
        pl.semaphore_signal(barrier, inc=1, device_id={"los": lax.rem(los + i, los_count)}, device_id_type=mesh)
    slab, rows, width = density.shape
    layers = slab * los_count
    tiles = width // LANES
    deep = 16

    def load(r):
        at = pl.ds(pl.multiple_of(r * deep, deep), deep)
        return pltpu.make_async_copy(density.at[:, at, :], raw.at[:, at, :], loads.at[r])

    for r in range(rows // deep):
        load(r).start()
    fetches = [
        pltpu.make_async_copy(source, target, local.at[i])
        for i, (source, target) in enumerate(
            ((refine_in, refine), (table_in, table), (forward_in, forward), (twist_in, twist))
        )
    ]
    for fetch in fetches:
        fetch.start()

    average = [0.5 * (weight_low[z] + weight_high[z]) for z in range(slab)]
    slope = [0.125 * (weight_high[z] - weight_low[z]) for z in range(slab)]
    blocks, coarse = refine.shape
    wide = width // coarse
    span = LANES * wide
    line = lax.broadcasted_iota(jnp.int32, (LANES, span), 0)
    column = lax.broadcasted_iota(jnp.int32, (LANES, span), 1)
    fetches[0].wait()
    stretch = jnp.where((column >= line * wide) & (column < line * wide + wide), 1.0, 0.0).astype(jnp.bfloat16)
    for h in range(coarse // LANES):
        flags = refine[:, h * LANES : (h + 1) * LANES].astype(jnp.float32).astype(jnp.bfloat16)
        grown = jnp.dot(flags, stretch, preferred_element_type=jnp.float32)
        for i in range(wide):
            marks[h * wide + i] = grown[:, i * LANES : (i + 1) * LANES]

    def fill(r, carry):
        load(r).wait()
        start = pl.multiple_of(r * deep, deep)
        into = pl.ds(pl.multiple_of(start + SUB, SUB), deep)
        for z in range(slab):
            for t in range(tiles):
                cells[z, t, into, :] = raw[z, pl.ds(start, deep), t * LANES : (t + 1) * LANES].astype(jnp.float32)
        return carry

    lax.fori_loop(0, rows // deep, fill, 0)
    pl.semaphore_wait(barrier, sky_count + los_count - 2)

    def hop(source, target, i, axis, me, count, shift):
        return pltpu.make_async_remote_copy(
            src_ref=source, dst_ref=target, send_sem=halo_s.at[i], recv_sem=halo_r.at[i],
            device_id={axis: lax.rem(me + shift, count)}, device_id_type=mesh,
        )

    onward = hop(density.at[slab - 1], below, 0, "los", los, los_count, 1)
    back = hop(density.at[0], above, 1, "los", los, los_count, los_count - 1)

    def rim(ref, i, lead):
        pieces = []
        for source, target, shift in ((SUB + rows - 1, SUB - 1, 1), (SUB, SUB + rows, sky_count - 1)):
            index = (slice(None),) * lead
            pieces.append(
                hop(
                    ref.at[index + (pl.ds(source, 1),)], ref.at[index + (pl.ds(target, 1),)],
                    i + len(pieces), "sky", sky, sky_count, shift,
                )
            )
        return pieces

    has_next, has_prior = los < los_count - 1, los > 0
    sides = rim(cells, 2, 2)
    for copy in sides:
        copy.start()
    pl.when(has_next)(onward.start)
    pl.when(has_prior)(back.start)

    lane8 = lax.broadcasted_iota(jnp.int32, (SUB, LANES), 1)
    lane_first, lane_last = lane8 == 0, lane8 == LANES - 1

    def chunk(r, carry):
        start = pl.multiple_of(r * SUB, SUB)
        at = pl.multiple_of(start + SUB, SUB)
        here, up, down = pl.ds(at, SUB), pl.ds(at - 1, SUB), pl.ds(at + 1, SUB)
        batch = 4
        for first in range(0, tiles, batch):
            ours = range(first, first + batch)
            total = [[None] * batch for _ in range(4)]

            def put(i, w, value):
                total[i][w] = value if total[i][w] is None else total[i][w] + value

            mid = [cells[0, t, here, :] for t in ours]
            step_z = [None] * batch
            for z in range(slab):
                prior = cells[z, (first - 1) % tiles, here, :]
                later = cells[z, (first + batch) % tiles, here, :]
                left = [pltpu.roll(v, LANES - 1, 1) for v in mid + [later]]
                right = [pltpu.roll(v, 1, 1) for v in [prior] + mid]
                for w, t in enumerate(ours):
                    v = mid[w]
                    put(0, w, average[z] * v)
                    put(2, w, average[z] * median0(cells[z, t, down, :] - v, v - cells[z, t, up, :]))
                    ahead = jnp.where(lane_last, left[w + 1], left[w])
                    behind = jnp.where(lane_first, right[w], right[w + 1])
                    put(3, w, average[z] * median0(ahead - v, v - behind))
                    if z < slab - 1:
                        above_v = cells[z + 1, t, here, :]
                        next_z = above_v - v
                        if z > 0:
                            put(1, w, slope[z] * median0(next_z, step_z[w]))
                        mid[w], step_z[w] = above_v, next_z
            for i in range(4):
                for w, t in enumerate(ours):
                    value = total[i][w]
                    sums[i, t, pl.ds(start, SUB), :] = jnp.zeros((SUB, LANES), jnp.float32) if value is None else value
        return carry

    lax.fori_loop(1, rows // SUB - 1, chunk, 0)
    for copy in sides:
        copy.wait()
    lax.fori_loop(0, 2, lambda i, carry: chunk(i * (rows // SUB - 1), carry), 0)

    def edge(z, inner, outer, sign):
        def add_edge(r, carry):
            start = pl.multiple_of(r * deep, deep)
            at = pl.ds(pl.multiple_of(start + SUB, SUB), deep)
            here = pl.ds(start, deep)
            for t in range(tiles):
                v = cells[z, t, at, :]
                u = outer[here, t * LANES : (t + 1) * LANES].astype(jnp.float32)
                sums[1, t, here, :] += (sign * slope[z]) * median0(cells[inner, t, at, :] - v, v - u)
            return carry

        lax.fori_loop(0, rows // deep, add_edge, 0)

    @pl.when(has_prior)
    def _():
        onward.wait_recv()
        edge(0, 1, below, 1.0)

    @pl.when(has_next)
    def _():
        back.wait_recv()
        edge(slab - 1, slab - 2, above, -1.0)

    def late(r, carry):
        start = pl.multiple_of(r * SUB, SUB)
        here = pl.ds(start, SUB)
        into = pl.ds(pl.multiple_of(start + SUB, SUB), SUB)
        known = {}

        def item(t):
            if t not in known:
                mark = marks[t, pl.ds(r, 1), :]
                base = sums[0, t, here, :]
                refined = mark * base
                rest[t, here, :] = base - refined
                f = refined + mark * sums[1, t, here, :]
                slant = mark * sums[3, t, here, :] * (1.0 / 32.0)
                g = mark * sums[2, t, here, :]
                e = 0.125 * f
                known[t] = (
                    f, g, pltpu.roll(e + slant, 1, 1), pltpu.roll(e - slant, LANES - 1, 1),
                    pltpu.roll(g, 1, 1), pltpu.roll(g, LANES - 1, 1),
                )
            return known[t]

        for t in range(tiles):
            one, two, three = item((t - 1) % tiles), item(t), item((t + 1) % tiles)
            smooth[t, into, :] = (
                0.75 * two[0] + jnp.where(lane_first, one[2], two[2]) + jnp.where(lane_last, three[3], two[3])
            )
            tilt[t, into, :] = 0.75 * two[1] + 0.125 * (
                jnp.where(lane_first, one[4], two[4]) + jnp.where(lane_last, three[5], two[5])
            )
        return carry

    lax.fori_loop(0, rows // SUB, lambda i, carry: late(lax.rem(i + rows // SUB - 1, rows // SUB), carry), 0)
    rims = rim(smooth, 4, 1) + rim(tilt, 6, 1)
    for copy in rims:
        copy.start()

    def finish(r, carry):
        start = pl.multiple_of(r * SUB, SUB)
        at = pl.multiple_of(start + SUB, SUB)
        here, up, down = pl.ds(at, SUB), pl.ds(at - 1, SUB), pl.ds(at + 1, SUB)
        into = pl.ds(start, SUB)
        parts = []
        for t in range(tiles):
            deposit = (
                rest[t, into, :]
                + 0.75 * smooth[t, here, :]
                + 0.125 * (smooth[t, up, :] + smooth[t, down, :])
                + (tilt[t, up, :] - tilt[t, down, :]) * (1.0 / 32.0)
            )
            parts.append((deposit, None))
        modes = fft_list(parts, -1.0)
        for c in range(tiles // 2):
            two = (modes[0][0], modes[tiles // 2][0]) if c == 0 else modes[c]
            relative = lax.rem(c // groups - los + los_count, los_count)
            for j in range(2):
                fold[relative, c % groups, j, into, :] = two[j]
        return carry

    lax.fori_loop(1, rows // SUB - 1, finish, 0)
    for copy in rims:
        copy.wait()
    lax.fori_loop(0, 2, lambda i, carry: finish(i * (rows // SUB - 1), carry), 0)

    def share(g, i):
        return pltpu.make_async_remote_copy(
            src_ref=hop_send.at[i - 1, g], dst_ref=hop_recv.at[los_count - 1 - i, g],
            send_sem=hs.at[i, g], recv_sem=hr.at[i, g],
            device_id={"los": lax.rem(los + i, los_count)}, device_id_type=mesh,
        )

    for g in range(groups):
        for i in range(1, los_count):
            re, im = fold[i, g, 0], fold[i, g, 1]
            if g == 0:
                words, level, wide = pack(re, im, re[0:1], True)
                hop_send[i - 1, g, rows + 1 : rows + 2, :] = wide
            else:
                words, level, _ = pack(re, im)
            hop_send[i - 1, g, 0:rows, :] = words
            hop_send[i - 1, g, rows : rows + 1, :] = level
            share(g, i).start()

    pair = 2
    part = LANES // sky_count
    each = groups // chunks
    count = each * part
    classes = length // LANES // 2
    half = LANES // 2

    def mode_of(kind, j):
        n = jnp.where(kind == 0, jnp.where(j < half, tiles * j, tiles * (j - half) + classes), kind + tiles * j)
        return jnp.where(n >= length // 2, n - length, n)

    def sky_copy(source, target, send, recv, i):
        peer = lax.rem(sky + i, sky_count)
        return pltpu.make_async_remote_copy(
            src_ref=source(peer), dst_ref=target, send_sem=send, recv_sem=recv,
            device_id={"sky": peer}, device_id_type=mesh,
        )

    def forward_copy(c, i):
        size = count + (2 if c == 0 else 1)
        return sky_copy(
            lambda peer: fsend.at[c, peer, pl.ds(0, size)], frecv.at[c, sky, pl.ds(0, size)],
            fs.at[c, i], fr.at[c, i], i,
        )

    def backward_copy(f, c, i):
        return sky_copy(
            lambda peer: bsend.at[f, c, peer, pl.ds(0, count + 1)], brecv.at[f, c, sky, pl.ds(0, count + 1)],
            bs.at[f, c, i], br.at[f, c, i], i,
        )

    def cross_copy(f, c, i):
        return pltpu.make_async_remote_copy(
            src_ref=brecv.at[f, c, :, pl.ds(0, count + 1)],
            dst_ref=cross.at[los_count - 1 - i, f, c, :, pl.ds(0, count + 1)],
            send_sem=xs.at[f, c, i], recv_sem=xr.at[f, c, i],
            device_id={"los": lax.rem(los + i, los_count)}, device_id_type=mesh,
        )

    order = lax.broadcasted_iota(jnp.int32, (LANES, rows), 0)
    for fetch in fetches[1:]:
        fetch.wait()
    for c in range(chunks):
        for g in range(c * each, (c + 1) * each):
            sides = [fold[0, g, j] for j in range(pair)]
            for i in range(1, los_count):
                share(g, i).wait_recv()
                slot = los_count - 1 - i
                re, im, step = unpack(hop_recv[slot, g, 0:rows, :], hop_recv[slot, g, rows : rows + 1, :])
                if g == 0:
                    re = re + hop_recv[slot, g, rows + 1 : rows + 2, :].astype(jnp.float32) * step
                sides = [sides[0] + re, sides[1] + im]
            kind = los * groups + g
            z = dot(table[kind], jnp.concatenate(sides, axis=1), ((1,), (1,)))
            n = jnp.maximum(jnp.abs(mode_of(kind, order)), 1).astype(jnp.float32)
            weight = lax.rsqrt(n)
            nyquist = (kind == 0) & (order == 0)
            spectra[g, 0] = z[:LANES] * weight
            spectra[g, 1] = z[LANES:] * jnp.where(nyquist, 1.0 / math.sqrt(length // 2), weight)
        for d in range(sky_count):
            re, im = [
                jnp.concatenate(
                    [spectra[g, j, d * part : (d + 1) * part, :] for g in range(c * each, (c + 1) * each)], axis=0
                )
                for j in range(pair)
            ]
            spare = None
            if c == 0:
                spare = re[0:1]
                re = jnp.where(lax.broadcasted_iota(jnp.int32, re.shape, 0) == 0, 0.0, re)
            words, level, wide = pack(re, im, spare)
            fsend[c, d, 0:count, :] = words
            fsend[c, d, count : count + 1, :] = level
            if c == 0:
                fsend[c, d, count + 1 : count + 2, :] = wide
        for i in range(1, sky_count):
            forward_copy(c, i).start()
        frecv[c, pl.ds(sky, 1)] = fsend[c, pl.ds(sky, 1)]

    unit = 2.0 * math.pi / length
    base = -2.0 / (unit * float(length) * float(length) * float(layers))

    def masks(c, shape):
        line = lax.broadcasted_iota(jnp.int32, shape, 0)
        packed = (line == 0) & (los == 0) & (sky == 0) if c == 0 else None
        return line, packed

    for c in range(chunks):
        extra = SUB if c == 0 else 0
        total = count + extra
        line, packed = masks(c, (total, rows))
        lane = lax.broadcasted_iota(jnp.int32, (total, rows), 1)
        n = mode_of(los * groups + c * each + line // part, sky * part + line % part)
        single = line >= count
        if c == 0:
            n = jnp.where(single, length // 2, n)
            single = single | packed
        ny = n.astype(jnp.float32)
        odd_y = jnp.where(n == length // 2, 0.0, ny)
        weight = jnp.where(single, base, 2.0 * base) * jnp.sqrt(jnp.maximum(jnp.abs(ny), 1.0))
        for k in range(sky_count):
            nx = k + sky_count * lane
            nx = jnp.where(nx >= length // 2, nx - length, nx)
            odd_x = jnp.where(nx == -(length // 2), 0, nx).astype(jnp.float32)
            square = nx.astype(jnp.float32) * nx.astype(jnp.float32) + ny * ny
            factor = jnp.where(square == 0.0, 0.0, weight / jnp.where(square == 0.0, 1.0, square))
            scales[c, 0, k, 0:total, :] = odd_x * factor
            scales[c, 1, k, 0:total, :] = odd_y * factor

    for c in range(chunks):
        extra = SUB if c == 0 else 0
        total = count + extra
        line, packed = masks(c, (total, rows))
        for i in range(1, sky_count):
            forward_copy(c, i).wait_recv()
        items = []
        for s in range(sky_count):
            re, im, step = unpack(frecv[c, s, 0:count, :], frecv[c, s, count : count + 1, :])
            if c == 0:
                wide = frecv[c, s, count + 1 : count + 2, :].astype(jnp.float32) * step
                re = jnp.where(line[:count] == 0, wide, re)
                zero = jnp.zeros((extra, rows), jnp.float32)
                re = jnp.concatenate([re, jnp.broadcast_to(im[0:1], (extra, rows))], axis=0)
                im = jnp.where(packed, 0.0, jnp.concatenate([im, zero], axis=0))
            items.append((re, im))
        items = fft_list(items, -1.0)
        turned = []
        for k, (re, im) in enumerate(items):
            co, si = twist[k, 0:1, :], twist[k, 1:2, :]
            turned.append(jnp.concatenate([re * co + im * si, im * co - re * si], axis=1))
        spectrum = dot(jnp.concatenate(turned, axis=0), forward[...], ((1,), (0,)))
        for f in range(2):
            fields = []
            for k in range(sky_count):
                here = spectrum[k * total : (k + 1) * total]
                scale = scales[c, f, k, 0:total, :]
                fields.append(jnp.concatenate([-scale * here[:, rows:], scale * here[:, :rows]], axis=1))
            values = dot(jnp.concatenate(fields, axis=0), forward[...], ((1,), (1,)))
            items = []
            for k in range(sky_count):
                here = values[k * total : (k + 1) * total]
                re, im = here[:, :rows], here[:, rows:]
                co, si = twist[k, 0:1, :], twist[k, 1:2, :]
                items.append((re * co - im * si, im * co + re * si))
            items = fft_list(items, 1.0)
            for s in range(sky_count):
                re, im = items[s]
                if c == 0:
                    im = jnp.where(packed[:count], jnp.broadcast_to(re[count : count + 1], (count, rows)), im[:count])
                    re = re[:count]
                words, level, _ = pack(re, im)
                bsend[f, c, s, 0:count, :] = words
                bsend[f, c, s, count : count + 1, :] = level
            for i in range(1, sky_count):
                backward_copy(f, c, i).start()
            brecv[f, c, pl.ds(sky, 1)] = bsend[f, c, pl.ds(sky, 1)]

    inner = out_x.shape[1] // LANES
    fresh = [True, True]

    def plane(f, c, block, owner):
        parts = [unpack(block[s, 0:count, :], block[s, count : count + 1, :]) for s in range(sky_count)]
        pieces = []
        for g in range(each):
            z = jnp.concatenate([p[j][g * part : (g + 1) * part] for j in range(pair) for p in parts], axis=0)
            kind = owner * groups + c * each + g
            both = dot(z, table[kind], ((0,), (0,)))
            pieces.append((kind, both[:, :LANES], both[:, LANES:]))
        for i in range(inner):
            at = 2 * (los * inner + i)
            tile = slice(i * LANES, (i + 1) * LANES)
            total = None if fresh[f] else outs[f][:, tile]
            for kind, one, two in pieces:
                term = mix[kind, at] * one + mix[kind, at + 1] * two
                total = term if total is None else total + term
            outs[f][:, tile] = total
        fresh[f] = False

    def arrive(f, c):
        for i in range(1, sky_count):
            backward_copy(f, c, i).wait_recv()
        for i in range(1, los_count):
            cross_copy(f, c, i).start()
        plane(f, c, brecv.at[f, c], los)

    def collect(f, c):
        for i in range(1, los_count):
            cross_copy(f, c, i).wait_recv()
            slot = los_count - 1 - i
            plane(f, c, cross.at[slot, f, c], lax.rem(los + los_count - i, los_count))

    steps = [(f, c) for c in range(chunks) for f in range(2)]
    for at, step in enumerate(steps):
        arrive(*step)
        if at:
            collect(*steps[at - 1])
    collect(*steps[-1])
    pl.when(has_next)(onward.wait_send)
    pl.when(has_prior)(back.wait_send)
    for g in range(groups):
        for i in range(1, los_count):
            share(g, i).wait_send()
    for c in range(chunks):
        for i in range(1, sky_count):
            forward_copy(c, i).wait_send()
            for f in range(2):
                backward_copy(f, c, i).wait_send()
        for f in range(2):
            for i in range(1, los_count):
                cross_copy(f, c, i).wait_send()


def call(kernel, shapes, specs, scratch=(), work=1, grid=(), types=jnp.float32, number=None):
    if not isinstance(types, tuple):
        types = jax.tree.map(lambda shape: types, shapes, is_leaf=lambda s: isinstance(s[0], int))
    return pl.pallas_call(
        kernel,
        grid=grid,
        out_shape=jax.tree.map(
            jax.ShapeDtypeStruct, shapes, types, is_leaf=lambda s: isinstance(s[0], int)
        ),
        in_specs=specs,
        out_specs=jax.tree.map(lambda shape: VMEM, shapes, is_leaf=lambda s: isinstance(s[0], int)),
        scratch_shapes=list(scratch),
        cost_estimate=pl.CostEstimate(flops=work, bytes_accessed=work, transcendentals=0),
        compiler_params=pltpu.CompilerParams(
            vmem_limit_bytes=60 * 1024 * 1024, collective_id=number, has_side_effects=number is not None
        ),
    )


def body(density, refine, weight_low, weight_high):
    los_count, sky_count = lax.axis_size("los"), lax.axis_size("sky")
    slab, rows, width = density.shape
    length = rows * sky_count
    tiles = width // LANES
    groups = tiles // 2 // los_count
    part = LANES // sky_count
    table = row_table(width)
    forward, twist = column_tables(length, sky_count)
    mix = tile_table(width)
    chunks = 2 if groups % 2 == 0 else 1
    peers = (sky_count, -(-(groups // chunks * part + 2) // SUB) * SUB, rows)
    scaled = (sky_count, groups // chunks * part + SUB, rows)
    dma = pltpu.SemaphoreType.DMA
    f32, i32 = jnp.float32, jnp.int32
    return pl.pallas_call(
        functools.partial(lens_kernel, length, los_count, sky_count, groups, chunks),
        out_shape=(jax.ShapeDtypeStruct((rows, width // los_count), f32),) * 2,
        in_specs=[ANY, ANY, SMEM, SMEM, ANY, ANY, ANY, SMEM],
        out_specs=(VMEM, VMEM),
        scratch_shapes=[
            pltpu.VMEM((slab, rows, width), density.dtype),
            pltpu.VMEM((slab, tiles, rows + 2 * SUB, LANES), f32),
            pltpu.VMEM((rows, width), density.dtype),
            pltpu.VMEM((rows, width), density.dtype),
            pltpu.VMEM((tiles, refine.shape[1], LANES), f32),
            pltpu.VMEM((4, tiles, rows, LANES), f32),
            pltpu.VMEM((tiles, rows, LANES), f32),
            pltpu.VMEM((tiles, rows + 2 * SUB, LANES), f32),
            pltpu.VMEM((tiles, rows + 2 * SUB, LANES), f32),
            pltpu.VMEM((los_count, groups, 2, rows, LANES), f32),
            pltpu.VMEM((los_count - 1, groups, rows + SUB, LANES), i32),
            pltpu.VMEM((los_count - 1, groups, rows + SUB, LANES), i32),
            pltpu.VMEM(table.shape, f32),
            pltpu.VMEM(forward.shape, f32),
            pltpu.VMEM(twist.shape, f32),
            pltpu.VMEM(refine.shape[1:], i32),
            pltpu.VMEM((groups, 2, LANES, rows), f32),
            pltpu.VMEM((chunks,) + peers, i32),
            pltpu.VMEM((chunks,) + peers, i32),
            pltpu.VMEM((2, chunks) + peers, i32),
            pltpu.VMEM((2, chunks) + peers, i32),
            pltpu.VMEM((los_count - 1, 2, chunks) + peers, i32),
            pltpu.VMEM((chunks, 2) + scaled, f32),
            dma((4,)),
            dma((rows // 16,)),
            dma((8,)),
            dma((8,)),
            dma((los_count, groups)),
            dma((los_count, groups)),
            dma((chunks, sky_count)),
            dma((chunks, sky_count)),
            dma((2, chunks, sky_count)),
            dma((2, chunks, sky_count)),
            dma((2, chunks, los_count)),
            dma((2, chunks, los_count)),
        ],
        compiler_params=pltpu.CompilerParams(
            vmem_limit_bytes=60 * 1024 * 1024, collective_id=0, has_side_effects=True
        ),
    )(density, refine[0], weight_low, weight_high, table, forward, twist, mix)


def solution(mesh):
    placed = (P("los", "sky", None), P("los", "sky", None), P("los"), P("los"))
    return jax.shard_map(
        body,
        mesh=mesh,
        in_specs=placed,
        out_specs=(P("sky", "los"), P("sky", "los")),
        check_vma=False,
    )
```

```python
import functools
import math

import jax
import jax.numpy as jnp
import numpy as np
from jax import lax
from jax.experimental import pallas as pl
from jax.experimental.pallas import tpu as pltpu
from jax.sharding import PartitionSpec as P

LANES = 128
SUB = 8
VMEM = pl.BlockSpec(memory_space=pltpu.VMEM)
SMEM = pl.BlockSpec(memory_space=pltpu.SMEM)
HBM = pl.BlockSpec(memory_space=pltpu.HBM)


def median0(a, b):
    return jnp.maximum(jnp.minimum(a, b), jnp.minimum(jnp.maximum(a, b), 0.0))


def add(p, q):
    im = q[1] if p[1] is None else (p[1] if q[1] is None else p[1] + q[1])
    return (p[0] + q[0], im)


def sub(p, q):
    if q[1] is None:
        return (p[0] - q[0], p[1])
    return (p[0] - q[0], -q[1] if p[1] is None else p[1] - q[1])


def turn(p, angle):
    c, s = math.cos(angle), math.sin(angle)
    re, im = p
    if abs(s) < 1e-12:
        return p if c > 0 else (-re, None if im is None else -im)
    if abs(c) < 1e-12:
        sign = 1.0 if s > 0 else -1.0
        if im is None:
            return (jnp.zeros_like(re), sign * re)
        return (-im, re) if s > 0 else (im, -re)
    if im is None:
        return (c * re, s * re)
    return (c * re - s * im, s * re + c * im)


def fft_list(items, flip):
    count = len(items)
    if count == 1:
        return items
    even = fft_list(items[0::2], flip)
    odd = fft_list(items[1::2], flip)
    first, second = [], []
    for k in range(count // 2):
        w = turn(odd[k], flip * 2.0 * math.pi * k / count)
        first.append(add(even[k], w))
        second.append(sub(even[k], w))
    return first + second


def row_table(width):
    tiles = width // LANES
    classes = tiles // 2
    half = LANES // 2
    t = np.arange(LANES)
    table = np.zeros((classes, 2 * LANES, 2 * LANES))

    def angles(n):
        return 2.0 * np.pi * ((n[:, None] * t[None, :]) % width) / width

    for c in range(classes):
        if c == 0:
            j = np.arange(half)
            low = angles(tiles * j)
            high = angles(tiles * j + classes)
            table[0, :half, :LANES] = np.cos(low)
            table[0, half:LANES, LANES:] = np.cos(high)
            table[0, LANES : LANES + half, :LANES] = -np.sin(low)
            table[0, LANES, :LANES] = np.cos(np.pi * t)
            table[0, LANES + half :, LANES:] = -np.sin(high)
        else:
            a = angles(c + tiles * np.arange(LANES))
            table[c, :LANES, :LANES] = np.cos(a)
            table[c, :LANES, LANES:] = np.sin(a)
            table[c, LANES:, :LANES] = -np.sin(a)
            table[c, LANES:, LANES:] = np.cos(a)
    return jnp.asarray(table, jnp.float32)


def tile_table(width):
    tiles = width // LANES
    classes = tiles // 2
    s = np.arange(tiles)
    table = np.zeros((classes, 2 * tiles))
    for c in range(classes):
        if c == 0:
            table[c, 0::2] = 1.0
            table[c, 1::2] = np.where(s % 2 == 0, 1.0, -1.0)
        else:
            table[c, 0::2] = np.cos(2.0 * np.pi * s * c / tiles)
            table[c, 1::2] = -np.sin(2.0 * np.pi * s * c / tiles)
    return jnp.asarray(table, jnp.float32)


def column_tables(length, sky):
    rows = length // sky
    t = np.arange(rows)
    a = 2.0 * np.pi * (t[:, None] * t[None, :] % rows) / rows
    c, s = np.cos(a), np.sin(a)
    forward = np.block([[c, -s], [s, c]])
    b = 2.0 * np.pi * (np.arange(sky)[:, None] * t[None, :]) / length
    twist = np.stack([np.cos(b), np.sin(b)], axis=1)
    return jnp.asarray(forward, jnp.float32), jnp.asarray(twist, jnp.float32)


def dot(a, b, dims):
    return lax.dot_general(
        a, b, (dims, ((), ())), precision=lax.Precision.HIGHEST, preferred_element_type=jnp.float32
    )


def pack(re, im, spare=None, centred=False):
    size = jnp.max(jnp.maximum(jnp.abs(re - spare if centred else re), jnp.abs(im)), axis=0, keepdims=True)
    if spare is not None:
        size = jnp.maximum(size, jnp.abs(spare) * (1.0 / 16384.0))
    level = jnp.ceil(jnp.log2(jnp.maximum(size, 1e-30) * (1.0 / 32700.0)) * 32.0)
    inverse = jnp.exp2(level * (-1.0 / 32.0))
    wide = None if spare is None else jnp.floor(spare * inverse + 0.5).astype(jnp.int32)
    if centred:
        re = re - wide.astype(jnp.float32) * jnp.exp2(level * (1.0 / 32.0))
    high = (re * inverse + 32768.5).astype(jnp.int32)
    low = (im * inverse + 32768.5).astype(jnp.int32)
    words = lax.shift_left(high, jnp.full_like(high, 16)) | low
    return words, level.astype(jnp.int32), wide


def unpack(words, level):
    step = jnp.exp2(level.astype(jnp.float32) * (1.0 / 32.0))
    high = lax.shift_right_logical(words, jnp.full_like(words, 16)).astype(jnp.float32)
    low = (words & 65535).astype(jnp.float32)
    return (high - 32768.0) * step, (low - 32768.0) * step, step


def lens_kernel(length, los_count, sky_count, groups, chunks, *refs):
    (
        density, refine_in, low_in, high_in, table_in, forward_in, twist_in, mix_in, out_x, out_y,
        raw, cells, below, above, marks, sums, rest, smooth, tilt, fold, hop_send, hop_recv,
        table, forward, twist, refine, weight_low, weight_high, mix, spectra, fsend, frecv, bsend, brecv, cross, scales, local,
        loads, plane_s, plane_r, halo_s, halo_r, hs, hr, fs, fr, bs, br, xs, xr,
    ) = refs
    outs = (out_x, out_y)
    mesh = pl.DeviceIdType.MESH
    los, sky = lax.axis_index("los"), lax.axis_index("sky")
    barrier = pltpu.get_barrier_semaphore()
    for i in range(1, sky_count):
        pl.semaphore_signal(barrier, inc=1, device_id={"sky": lax.rem(sky + i, sky_count)}, device_id_type=mesh)
    for i in range(1, los_count):
        pl.semaphore_signal(barrier, inc=1, device_id={"los": lax.rem(los + i, los_count)}, device_id_type=mesh)
    slab, rows, width = density.shape
    layers = slab * los_count
    tiles = width // LANES
    deep = 16

    def load(r):
        at = pl.ds(pl.multiple_of(r * deep, deep), deep)
        return pltpu.make_async_copy(density.at[:, at, :], raw.at[:, at, :], loads.at[r])

    for r in range(rows // deep):
        load(r).start()
    fetches = [
        pltpu.make_async_copy(source, target, local.at[i])
        for i, (source, target) in enumerate(
            (
                (refine_in, refine), (low_in, weight_low), (high_in, weight_high),
                (table_in, table), (forward_in, forward), (twist_in, twist), (mix_in, mix),
            )
        )
    ]
    for fetch in fetches:
        fetch.start()

    for fetch in fetches[:3]:
        fetch.wait()
    average = [0.5 * (weight_low[z] + weight_high[z]) for z in range(slab)]
    slope = [0.125 * (weight_high[z] - weight_low[z]) for z in range(slab)]
    blocks, coarse = refine.shape
    wide = width // coarse
    span = LANES * wide
    line = lax.broadcasted_iota(jnp.int32, (LANES, span), 0)
    column = lax.broadcasted_iota(jnp.int32, (LANES, span), 1)
    stretch = jnp.where((column >= line * wide) & (column < line * wide + wide), 1.0, 0.0).astype(jnp.bfloat16)
    for h in range(coarse // LANES):
        flags = refine[:, h * LANES : (h + 1) * LANES].astype(jnp.float32).astype(jnp.bfloat16)
        grown = jnp.dot(flags, stretch, preferred_element_type=jnp.float32)
        for i in range(wide):
            marks[h * wide + i] = grown[:, i * LANES : (i + 1) * LANES]

    pieces = plane_s.shape[1]
    band = rows // pieces
    has_next, has_prior = los < los_count - 1, los > 0

    def beside(i, p):
        at = pl.ds(p * band, band)
        return pltpu.make_async_remote_copy(
            src_ref=density.at[slab - 1 if i == 0 else 0, at, :],
            dst_ref=(below if i == 0 else above).at[at, :],
            send_sem=plane_s.at[i, p], recv_sem=plane_r.at[i, p],
            device_id={"los": lax.rem(los + (1 if i == 0 else los_count - 1), los_count)}, device_id_type=mesh,
        )

    outside_in = [0, pieces - 1] + list(range(1, pieces - 1))
    pl.semaphore_wait(barrier, sky_count + los_count - 2)
    for p in outside_in:
        pl.when(has_next)(beside(0, p).start)
        pl.when(has_prior)(beside(1, p).start)

    def fill(r, carry):
        load(r).wait()
        start = pl.multiple_of(r * deep, deep)
        into = pl.ds(pl.multiple_of(start + SUB, SUB), deep)
        for z in range(slab):
            for t in range(tiles):
                cells[z, t, into, :] = raw[z, pl.ds(start, deep), t * LANES : (t + 1) * LANES].astype(jnp.float32)
        return carry

    lax.fori_loop(0, rows // deep, fill, 0)

    def hop(source, target, i, axis, me, count, shift):
        return pltpu.make_async_remote_copy(
            src_ref=source, dst_ref=target, send_sem=halo_s.at[i], recv_sem=halo_r.at[i],
            device_id={axis: lax.rem(me + shift, count)}, device_id_type=mesh,
        )

    def rim(ref, i, lead):
        both = []
        for source, target, shift in ((SUB + rows - 1, SUB - 1, 1), (SUB, SUB + rows, sky_count - 1)):
            index = (slice(None),) * lead
            both.append(
                hop(
                    ref.at[index + (pl.ds(source, 1),)], ref.at[index + (pl.ds(target, 1),)],
                    i + len(both), "sky", sky, sky_count, shift,
                )
            )
        return both

    sides = rim(cells, 0, 2)
    for copy in sides:
        copy.start()

    lane8 = lax.broadcasted_iota(jnp.int32, (SUB, LANES), 1)
    lane_first, lane_last = lane8 == 0, lane8 == LANES - 1

    def chunk(r, carry):
        start = pl.multiple_of(r * SUB, SUB)
        at = pl.multiple_of(start + SUB, SUB)
        here, up, down = pl.ds(at, SUB), pl.ds(at - 1, SUB), pl.ds(at + 1, SUB)
        batch = 4
        for first in range(0, tiles, batch):
            ours = range(first, first + batch)
            total = [[None] * batch for _ in range(4)]

            def put(i, w, value):
                total[i][w] = value if total[i][w] is None else total[i][w] + value

            mid = [cells[0, t, here, :] for t in ours]
            step_z = [None] * batch
            for z in range(slab):
                prior = cells[z, (first - 1) % tiles, here, :]
                later = cells[z, (first + batch) % tiles, here, :]
                left = [pltpu.roll(v, LANES - 1, 1) for v in mid + [later]]
                right = [pltpu.roll(v, 1, 1) for v in [prior] + mid]
                for w, t in enumerate(ours):
                    v = mid[w]
                    put(0, w, average[z] * v)
                    put(2, w, average[z] * median0(cells[z, t, down, :] - v, v - cells[z, t, up, :]))
                    ahead = jnp.where(lane_last, left[w + 1], left[w])
                    behind = jnp.where(lane_first, right[w], right[w + 1])
                    put(3, w, average[z] * median0(ahead - v, v - behind))
                    if z < slab - 1:
                        above_v = cells[z + 1, t, here, :]
                        next_z = above_v - v
                        if z > 0:
                            put(1, w, slope[z] * median0(next_z, step_z[w]))
                        mid[w], step_z[w] = above_v, next_z
            for i in range(4):
                for w, t in enumerate(ours):
                    value = total[i][w]
                    sums[i, t, pl.ds(start, SUB), :] = jnp.zeros((SUB, LANES), jnp.float32) if value is None else value
        return carry

    lax.fori_loop(1, rows // SUB - 1, chunk, 0)
    for copy in sides:
        copy.wait()
    lax.fori_loop(0, 2, lambda i, carry: chunk(i * (rows // SUB - 1), carry), 0)

    def edge(p, z, inner, outer, sign):
        def add_edge(r, carry):
            start = pl.multiple_of(r * deep, deep)
            at = pl.ds(pl.multiple_of(start + SUB, SUB), deep)
            here = pl.ds(start, deep)
            for t in range(tiles):
                v = cells[z, t, at, :]
                u = outer[here, t * LANES : (t + 1) * LANES].astype(jnp.float32)
                sums[1, t, here, :] += (sign * slope[z]) * median0(cells[inner, t, at, :] - v, v - u)
            return carry

        lax.fori_loop(p * band // deep, (p + 1) * band // deep, add_edge, 0)

    def late(r, carry):
        start = pl.multiple_of(r * SUB, SUB)
        here = pl.ds(start, SUB)
        into = pl.ds(pl.multiple_of(start + SUB, SUB), SUB)
        known = {}

        def item(t):
            if t not in known:
                mark = marks[t, pl.ds(r, 1), :]
                base = sums[0, t, here, :]
                refined = mark * base
                rest[t, here, :] = base - refined
                f = refined + mark * sums[1, t, here, :]
                slant = mark * sums[3, t, here, :] * (1.0 / 32.0)
                g = mark * sums[2, t, here, :]
                e = 0.125 * f
                known[t] = (
                    f, g, pltpu.roll(e + slant, 1, 1), pltpu.roll(e - slant, LANES - 1, 1),
                    pltpu.roll(g, 1, 1), pltpu.roll(g, LANES - 1, 1),
                )
            return known[t]

        for t in range(tiles):
            one, two, three = item((t - 1) % tiles), item(t), item((t + 1) % tiles)
            smooth[t, into, :] = (
                0.75 * two[0] + jnp.where(lane_first, one[2], two[2]) + jnp.where(lane_last, three[3], two[3])
            )
            tilt[t, into, :] = 0.75 * two[1] + 0.125 * (
                jnp.where(lane_first, one[4], two[4]) + jnp.where(lane_last, three[5], two[5])
            )
        return carry

    rims = rim(smooth, 2, 1) + rim(tilt, 4, 1)
    for done, p in enumerate(outside_in):

        @pl.when(has_prior)
        def _():
            beside(0, p).wait_recv()
            edge(p, 0, 1, below, 1.0)

        @pl.when(has_next)
        def _():
            beside(1, p).wait_recv()
            edge(p, slab - 1, slab - 2, above, -1.0)

        lax.fori_loop(p * band // SUB, (p + 1) * band // SUB, late, 0)
        if done == 1:
            for copy in rims:
                copy.start()

    def finish(r, carry):
        start = pl.multiple_of(r * SUB, SUB)
        at = pl.multiple_of(start + SUB, SUB)
        here, up, down = pl.ds(at, SUB), pl.ds(at - 1, SUB), pl.ds(at + 1, SUB)
        into = pl.ds(start, SUB)
        parts = []
        for t in range(tiles):
            deposit = (
                rest[t, into, :]
                + 0.75 * smooth[t, here, :]
                + 0.125 * (smooth[t, up, :] + smooth[t, down, :])
                + (tilt[t, up, :] - tilt[t, down, :]) * (1.0 / 32.0)
            )
            parts.append((deposit, None))
        modes = fft_list(parts, -1.0)
        for c in range(tiles // 2):
            two = (modes[0][0], modes[tiles // 2][0]) if c == 0 else modes[c]
            relative = lax.rem(c // groups - los + los_count, los_count)
            for j in range(2):
                fold[relative, c % groups, j, into, :] = two[j]
        return carry

    lax.fori_loop(1, rows // SUB - 1, finish, 0)
    for copy in rims:
        copy.wait()
    lax.fori_loop(0, 2, lambda i, carry: finish(i * (rows // SUB - 1), carry), 0)

    def share(g, i):
        return pltpu.make_async_remote_copy(
            src_ref=hop_send.at[i - 1, g], dst_ref=hop_recv.at[los_count - 1 - i, g],
            send_sem=hs.at[i, g], recv_sem=hr.at[i, g],
            device_id={"los": lax.rem(los + i, los_count)}, device_id_type=mesh,
        )

    for g in range(groups):
        for i in range(1, los_count):
            re, im = fold[i, g, 0], fold[i, g, 1]
            if g == 0:
                words, level, wide = pack(re, im, re[0:1], True)
                hop_send[i - 1, g, rows + 1 : rows + 2, :] = wide
            else:
                words, level, _ = pack(re, im)
            hop_send[i - 1, g, 0:rows, :] = words
            hop_send[i - 1, g, rows : rows + 1, :] = level
            share(g, i).start()

    pair = 2
    part = LANES // sky_count
    each = groups // chunks
    count = each * part
    classes = length // LANES // 2
    half = LANES // 2

    def mode_of(kind, j):
        n = jnp.where(kind == 0, jnp.where(j < half, tiles * j, tiles * (j - half) + classes), kind + tiles * j)
        return jnp.where(n >= length // 2, n - length, n)

    def sky_copy(source, target, send, recv, i):
        peer = lax.rem(sky + i, sky_count)
        return pltpu.make_async_remote_copy(
            src_ref=source(peer), dst_ref=target, send_sem=send, recv_sem=recv,
            device_id={"sky": peer}, device_id_type=mesh,
        )

    def forward_copy(c, i):
        size = count + (2 if c == 0 else 1)
        return sky_copy(
            lambda peer: fsend.at[c, peer, pl.ds(0, size)], frecv.at[c, sky, pl.ds(0, size)],
            fs.at[c], fr.at[c], i,
        )

    def backward_copy(f, c, i):
        return sky_copy(
            lambda peer: bsend.at[f, c, peer, pl.ds(0, count + 1)], brecv.at[f, c, sky, pl.ds(0, count + 1)],
            bs.at[f, c], br.at[f, c], i,
        )

    def drain(ref, size, semaphore):
        part_of = ref.at[pl.ds(0, sky_count - 1), pl.ds(0, size)]
        pltpu.make_async_copy(part_of, part_of, semaphore).wait()

    def cross_copy(f, c, i):
        return pltpu.make_async_remote_copy(
            src_ref=brecv.at[f, c, :, pl.ds(0, count + 1)],
            dst_ref=cross.at[los_count - 1 - i, f, c, :, pl.ds(0, count + 1)],
            send_sem=xs.at[f, c, i], recv_sem=xr.at[f, c, i],
            device_id={"los": lax.rem(los + i, los_count)}, device_id_type=mesh,
        )

    unit = 2.0 * math.pi / length
    base = -2.0 / (unit * float(length) * float(length) * float(layers))

    def masks(c, shape):
        line = lax.broadcasted_iota(jnp.int32, shape, 0)
        packed = (line == 0) & (los == 0) & (sky == 0) if c == 0 else None
        return line, packed

    for c in range(chunks):
        extra = SUB if c == 0 else 0
        total = count + extra
        line, packed = masks(c, (total, rows))
        lane = lax.broadcasted_iota(jnp.int32, (total, rows), 1)
        n = mode_of(los * groups + c * each + line // part, sky * part + line % part)
        single = line >= count
        if c == 0:
            n = jnp.where(single, length // 2, n)
            single = single | packed
        ny = n.astype(jnp.float32)
        odd_y = jnp.where(n == length // 2, 0.0, ny)
        weight = jnp.where(single, base, 2.0 * base) * jnp.sqrt(jnp.maximum(jnp.abs(ny), 1.0))
        for k in range(sky_count):
            nx = k + sky_count * lane
            nx = jnp.where(nx >= length // 2, nx - length, nx)
            odd_x = jnp.where(nx == -(length // 2), 0, nx).astype(jnp.float32)
            square = nx.astype(jnp.float32) * nx.astype(jnp.float32) + ny * ny
            factor = jnp.where(square == 0.0, 0.0, weight / jnp.where(square == 0.0, 1.0, square))
            scales[c, 0, k, 0:total, :] = odd_x * factor
            scales[c, 1, k, 0:total, :] = odd_y * factor

    order = lax.broadcasted_iota(jnp.int32, (LANES, rows), 0)
    for fetch in fetches[3:]:
        fetch.wait()
    for c in range(chunks):
        for g in range(c * each, (c + 1) * each):
            sides = [fold[0, g, j] for j in range(pair)]
            for i in range(1, los_count):
                share(g, i).wait_recv()
                slot = los_count - 1 - i
                re, im, step = unpack(hop_recv[slot, g, 0:rows, :], hop_recv[slot, g, rows : rows + 1, :])
                if g == 0:
                    re = re + hop_recv[slot, g, rows + 1 : rows + 2, :].astype(jnp.float32) * step
                sides = [sides[0] + re, sides[1] + im]
            kind = los * groups + g
            z = dot(table[kind], jnp.concatenate(sides, axis=1), ((1,), (1,)))
            n = jnp.maximum(jnp.abs(mode_of(kind, order)), 1).astype(jnp.float32)
            weight = lax.rsqrt(n)
            nyquist = (kind == 0) & (order == 0)
            spectra[g, 0] = z[:LANES] * weight
            spectra[g, 1] = z[LANES:] * jnp.where(nyquist, 1.0 / math.sqrt(length // 2), weight)
        for d in range(sky_count):
            re, im = [
                jnp.concatenate(
                    [spectra[g, j, d * part : (d + 1) * part, :] for g in range(c * each, (c + 1) * each)], axis=0
                )
                for j in range(pair)
            ]
            spare = None
            if c == 0:
                spare = re[0:1]
                re = jnp.where(lax.broadcasted_iota(jnp.int32, re.shape, 0) == 0, 0.0, re)
            words, level, wide = pack(re, im, spare)
            fsend[c, d, 0:count, :] = words
            fsend[c, d, count : count + 1, :] = level
            if c == 0:
                fsend[c, d, count + 1 : count + 2, :] = wide
        for i in range(1, sky_count):
            forward_copy(c, i).start()
        frecv[c, pl.ds(sky, 1)] = fsend[c, pl.ds(sky, 1)]

    def relay(f, c):
        drain(brecv.at[f, c], count + 1, br.at[f, c])
        for i in range(1, los_count):
            cross_copy(f, c, i).start()

    for c in range(chunks):
        extra = SUB if c == 0 else 0
        total = count + extra
        line, packed = masks(c, (total, rows))
        drain(frecv.at[c], count + (2 if c == 0 else 1), fr.at[c])
        items = []
        for s in range(sky_count):
            re, im, step = unpack(frecv[c, s, 0:count, :], frecv[c, s, count : count + 1, :])
            if c == 0:
                wide = frecv[c, s, count + 1 : count + 2, :].astype(jnp.float32) * step
                re = jnp.where(line[:count] == 0, wide, re)
                zero = jnp.zeros((extra, rows), jnp.float32)
                re = jnp.concatenate([re, jnp.broadcast_to(im[0:1], (extra, rows))], axis=0)
                im = jnp.where(packed, 0.0, jnp.concatenate([im, zero], axis=0))
            items.append((re, im))
        items = fft_list(items, -1.0)
        turned = []
        for k, (re, im) in enumerate(items):
            co, si = twist[k, 0:1, :], twist[k, 1:2, :]
            turned.append(jnp.concatenate([re * co + im * si, im * co - re * si], axis=1))
        spectrum = dot(jnp.concatenate(turned, axis=0), forward[...], ((1,), (0,)))
        for f in range(2):
            fields = []
            for k in range(sky_count):
                here = spectrum[k * total : (k + 1) * total]
                scale = scales[c, f, k, 0:total, :]
                fields.append(jnp.concatenate([-scale * here[:, rows:], scale * here[:, :rows]], axis=1))
            values = dot(jnp.concatenate(fields, axis=0), forward[...], ((1,), (1,)))
            items = []
            for k in range(sky_count):
                here = values[k * total : (k + 1) * total]
                re, im = here[:, :rows], here[:, rows:]
                co, si = twist[k, 0:1, :], twist[k, 1:2, :]
                items.append((re * co - im * si, im * co + re * si))
            items = fft_list(items, 1.0)
            for s in range(sky_count):
                re, im = items[s]
                if c == 0:
                    im = jnp.where(packed[:count], jnp.broadcast_to(re[count : count + 1], (count, rows)), im[:count])
                    re = re[:count]
                words, level, _ = pack(re, im)
                bsend[f, c, s, 0:count, :] = words
                bsend[f, c, s, count : count + 1, :] = level
            for i in range(1, sky_count):
                backward_copy(f, c, i).start()
            brecv[f, c, pl.ds(sky, 1)] = bsend[f, c, pl.ds(sky, 1)]
            if c:
                relay(f, c - 1)

    inner = out_x.shape[1] // LANES
    fresh = [True, True]

    def plane(f, c, block, owner):
        parts = [unpack(block[s, 0:count, :], block[s, count : count + 1, :]) for s in range(sky_count)]
        pieces = []
        for g in range(each):
            z = jnp.concatenate([p[j][g * part : (g + 1) * part] for j in range(pair) for p in parts], axis=0)
            kind = owner * groups + c * each + g
            both = dot(z, table[kind], ((0,), (0,)))
            pieces.append((kind, both[:, :LANES], both[:, LANES:]))
        for i in range(inner):
            tile = slice(i * LANES, (i + 1) * LANES)
            total = None if fresh[f] else outs[f][:, tile]
            for kind, one, two in pieces:
                at = 2 * (kind * tiles + los * inner + i)
                term = mix[at] * one + mix[at + 1] * two
                total = term if total is None else total + term
            outs[f][:, tile] = total
        fresh[f] = False


    def collect(f, c):
        for i in range(1, los_count):
            cross_copy(f, c, i).wait_recv()
            slot = los_count - 1 - i
            plane(f, c, cross.at[slot, f, c], lax.rem(los + los_count - i, los_count))

    def own(f, c):
        plane(f, c, brecv.at[f, c], los)

    end = chunks - 1
    for c in range(end):
        own(0, c)
        own(1, c)
        collect(0, c)
        if c == end - 1:
            relay(0, end)
        collect(1, c)
    if not end:
        relay(0, end)
    relay(1, end)
    own(0, end)
    own(1, end)
    collect(0, end)
    collect(1, end)
    for p in range(pieces):
        pl.when(has_next)(beside(0, p).wait_send)
        pl.when(has_prior)(beside(1, p).wait_send)
    for g in range(groups):
        for i in range(1, los_count):
            share(g, i).wait_send()
    for c in range(chunks):
        drain(fsend.at[c], count + (2 if c == 0 else 1), fs.at[c])
        for f in range(2):
            drain(bsend.at[f, c], count + 1, bs.at[f, c])
        for f in range(2):
            for i in range(1, los_count):
                cross_copy(f, c, i).wait_send()


def body(density, refine, weight_low, weight_high):
    los_count, sky_count = lax.axis_size("los"), lax.axis_size("sky")
    slab, rows, width = density.shape
    length = rows * sky_count
    tiles = width // LANES
    groups = tiles // 2 // los_count
    part = LANES // sky_count
    table = row_table(width)
    forward, twist = column_tables(length, sky_count)
    mix = tile_table(width).reshape(-1)
    chunks = 2 if groups % 2 == 0 else 1
    peers = (sky_count, -(-(groups // chunks * part + 2) // SUB) * SUB, rows)
    scaled = (sky_count, groups // chunks * part + SUB, rows)
    operands = (density, refine[0], weight_low, weight_high, table, forward, twist, mix)
    dma = pltpu.SemaphoreType.DMA
    f32, i32 = jnp.float32, jnp.int32
    return pl.pallas_call(
        functools.partial(lens_kernel, length, los_count, sky_count, groups, chunks),
        out_shape=(jax.ShapeDtypeStruct((rows, width // los_count), f32),) * 2,
        in_specs=[HBM] * 8,
        out_specs=(VMEM, VMEM),
        scratch_shapes=[
            pltpu.VMEM((slab, rows, width), density.dtype),
            pltpu.VMEM((slab, tiles, rows + 2 * SUB, LANES), f32),
            pltpu.VMEM((rows, width), density.dtype),
            pltpu.VMEM((rows, width), density.dtype),
            pltpu.VMEM((tiles, refine.shape[1], LANES), f32),
            pltpu.VMEM((4, tiles, rows, LANES), f32),
            pltpu.VMEM((tiles, rows, LANES), f32),
            pltpu.VMEM((tiles, rows + 2 * SUB, LANES), f32),
            pltpu.VMEM((tiles, rows + 2 * SUB, LANES), f32),
            pltpu.VMEM((los_count, groups, 2, rows, LANES), f32),
            pltpu.VMEM((los_count - 1, groups, rows + SUB, LANES), i32),
            pltpu.VMEM((los_count - 1, groups, rows + SUB, LANES), i32),
            pltpu.VMEM(table.shape, f32),
            pltpu.VMEM(forward.shape, f32),
            pltpu.VMEM(twist.shape, f32),
            pltpu.VMEM(refine.shape[1:], i32),
            pltpu.SMEM((slab,), f32),
            pltpu.SMEM((slab,), f32),
            pltpu.SMEM(mix.shape, f32),
            pltpu.VMEM((groups, 2, LANES, rows), f32),
            pltpu.VMEM((chunks,) + peers, i32),
            pltpu.VMEM((chunks,) + peers, i32),
            pltpu.VMEM((2, chunks) + peers, i32),
            pltpu.VMEM((2, chunks) + peers, i32),
            pltpu.VMEM((los_count - 1, 2, chunks) + peers, i32),
            pltpu.VMEM((chunks, 2) + scaled, f32),
            dma((7,)),
            dma((rows // 16,)),
            dma((2, 4)),
            dma((2, 4)),
            dma((6,)),
            dma((6,)),
            dma((los_count, groups)),
            dma((los_count, groups)),
            dma((chunks,)),
            dma((chunks,)),
            dma((2, chunks)),
            dma((2, chunks)),
            dma((2, chunks, los_count)),
            dma((2, chunks, los_count)),
        ],
        compiler_params=pltpu.CompilerParams(
            vmem_limit_bytes=48 * 1024 * 1024, collective_id=0, has_side_effects=True
        ),
    )(*[pltpu.with_memory_space_constraint(x, pltpu.HBM) for x in operands])


def solution(mesh):
    placed = (P("los", "sky", None), P("los", "sky", None), P("los"), P("los"))
    return jax.shard_map(
        body,
        mesh=mesh,
        in_specs=placed,
        out_specs=(P("sky", "los"), P("sky", "los")),
        check_vma=False,
    )
```

```python
import functools
import math

import jax
import jax.numpy as jnp
import numpy as np
from jax import lax
from jax.experimental import pallas as pl
from jax.experimental.pallas import tpu as pltpu
from jax.sharding import PartitionSpec as P

LANES = 128
SUB = 8
VMEM = pl.BlockSpec(memory_space=pltpu.VMEM)
SMEM = pl.BlockSpec(memory_space=pltpu.SMEM)
ANY = pl.BlockSpec(memory_space=pl.ANY)
HBM = pl.BlockSpec(memory_space=pltpu.HBM)


def median0(a, b):
    return jnp.maximum(jnp.minimum(a, b), jnp.minimum(jnp.maximum(a, b), 0.0))


def add(p, q):
    im = q[1] if p[1] is None else (p[1] if q[1] is None else p[1] + q[1])
    return (p[0] + q[0], im)


def sub(p, q):
    if q[1] is None:
        return (p[0] - q[0], p[1])
    return (p[0] - q[0], -q[1] if p[1] is None else p[1] - q[1])


def turn(p, angle):
    c, s = math.cos(angle), math.sin(angle)
    re, im = p
    if abs(s) < 1e-12:
        return p if c > 0 else (-re, None if im is None else -im)
    if abs(c) < 1e-12:
        sign = 1.0 if s > 0 else -1.0
        if im is None:
            return (jnp.zeros_like(re), sign * re)
        return (-im, re) if s > 0 else (im, -re)
    if im is None:
        return (c * re, s * re)
    return (c * re - s * im, s * re + c * im)


def fft_list(items, flip):
    count = len(items)
    if count == 1:
        return items
    even = fft_list(items[0::2], flip)
    odd = fft_list(items[1::2], flip)
    first, second = [], []
    for k in range(count // 2):
        w = turn(odd[k], flip * 2.0 * math.pi * k / count)
        first.append(add(even[k], w))
        second.append(sub(even[k], w))
    return first + second


def row_table(width):
    tiles = width // LANES
    classes = tiles // 2
    half = LANES // 2
    t = np.arange(LANES)
    table = np.zeros((classes, 2 * LANES, 2 * LANES))

    def angles(n):
        return 2.0 * np.pi * ((n[:, None] * t[None, :]) % width) / width

    for c in range(classes):
        if c == 0:
            j = np.arange(half)
            low = angles(tiles * j)
            high = angles(tiles * j + classes)
            table[0, :half, :LANES] = np.cos(low)
            table[0, half:LANES, LANES:] = np.cos(high)
            table[0, LANES : LANES + half, :LANES] = -np.sin(low)
            table[0, LANES, :LANES] = np.cos(np.pi * t)
            table[0, LANES + half :, LANES:] = -np.sin(high)
        else:
            a = angles(c + tiles * np.arange(LANES))
            table[c, :LANES, :LANES] = np.cos(a)
            table[c, :LANES, LANES:] = np.sin(a)
            table[c, LANES:, :LANES] = -np.sin(a)
            table[c, LANES:, LANES:] = np.cos(a)
    return jnp.asarray(table, jnp.float32)


def tile_table(width):
    tiles = width // LANES
    classes = tiles // 2
    s = np.arange(tiles)
    table = np.zeros((classes, 2 * tiles))
    for c in range(classes):
        if c == 0:
            table[c, 0::2] = 1.0
            table[c, 1::2] = np.where(s % 2 == 0, 1.0, -1.0)
        else:
            table[c, 0::2] = np.cos(2.0 * np.pi * s * c / tiles)
            table[c, 1::2] = -np.sin(2.0 * np.pi * s * c / tiles)
    return jnp.asarray(table, jnp.float32)


def column_tables(length, sky):
    rows = length // sky
    t = np.arange(rows)
    a = 2.0 * np.pi * (t[:, None] * t[None, :] % rows) / rows
    c, s = np.cos(a), np.sin(a)
    forward = np.block([[c, -s], [s, c]])
    b = 2.0 * np.pi * (np.arange(sky)[:, None] * t[None, :]) / length
    twist = np.stack([np.cos(b), np.sin(b)], axis=1)
    return jnp.asarray(forward, jnp.float32), jnp.asarray(twist, jnp.float32)


def dot(a, b, dims):
    return lax.dot_general(
        a, b, (dims, ((), ())), precision=lax.Precision.HIGHEST, preferred_element_type=jnp.float32
    )


def pack(re, im, spare=None, centred=False):
    size = jnp.max(jnp.maximum(jnp.abs(re - spare if centred else re), jnp.abs(im)), axis=0, keepdims=True)
    if spare is not None:
        size = jnp.maximum(size, jnp.abs(spare) * (1.0 / 16384.0))
    level = jnp.ceil(jnp.log2(jnp.maximum(size, 1e-30) * (1.0 / 32700.0)) * 32.0)
    inverse = jnp.exp2(level * (-1.0 / 32.0))
    wide = None if spare is None else jnp.floor(spare * inverse + 0.5).astype(jnp.int32)
    if centred:
        re = re - wide.astype(jnp.float32) * jnp.exp2(level * (1.0 / 32.0))
    high = (re * inverse + 32768.5).astype(jnp.int32)
    low = (im * inverse + 32768.5).astype(jnp.int32)
    words = lax.shift_left(high, jnp.full_like(high, 16)) | low
    return words, level.astype(jnp.int32), wide


def unpack(words, level):
    step = jnp.exp2(level.astype(jnp.float32) * (1.0 / 32.0))
    high = lax.shift_right_logical(words, jnp.full_like(words, 16)).astype(jnp.float32)
    low = (words & 65535).astype(jnp.float32)
    return (high - 32768.0) * step, (low - 32768.0) * step, step


def lens_kernel(length, los_count, sky_count, groups, chunks, *refs):
    (
        density, refine_in, low_in, high_in, table_in, forward_in, twist_in, mix_in, out_x, out_y,
        raw, cells, below, above, marks, sums, rest, smooth, tilt, fold, hop_send, hop_recv,
        table, forward, twist, refine, weight_low, weight_high, mix, spectra, fsend, frecv, bsend, brecv, cross, scales, local,
        loads, plane_s, plane_r, halo_s, halo_r, hs, hr, fs, fr, bs, br, xs, xr,
    ) = refs
    outs = (out_x, out_y)
    mesh = pl.DeviceIdType.MESH
    los, sky = lax.axis_index("los"), lax.axis_index("sky")
    barrier = pltpu.get_barrier_semaphore()
    for i in range(1, sky_count):
        pl.semaphore_signal(barrier, inc=1, device_id={"sky": lax.rem(sky + i, sky_count)}, device_id_type=mesh)
    for i in range(1, los_count):
        pl.semaphore_signal(barrier, inc=1, device_id={"los": lax.rem(los + i, los_count)}, device_id_type=mesh)
    slab, rows, width = density.shape
    layers = slab * los_count
    tiles = width // LANES
    deep = 16

    def load(r):
        at = pl.ds(pl.multiple_of(r * deep, deep), deep)
        return pltpu.make_async_copy(density.at[:, at, :], raw.at[:, at, :], loads.at[r])

    strips = rows // deep
    for r in [0, strips - 1] + list(range(1, strips - 1)):
        load(r).start()
    fetches = [
        pltpu.make_async_copy(source, target, local.at[i])
        for i, (source, target) in enumerate(
            (
                (refine_in, refine), (low_in, weight_low), (high_in, weight_high),
                (table_in, table), (forward_in, forward), (twist_in, twist), (mix_in, mix),
            )
        )
    ]
    for fetch in fetches[:3]:
        fetch.start()

    for fetch in fetches[:3]:
        fetch.wait()
    average = [0.5 * (weight_low[z] + weight_high[z]) for z in range(slab)]
    slope = [0.125 * (weight_high[z] - weight_low[z]) for z in range(slab)]
    blocks, coarse = refine.shape
    wide = width // coarse
    span = LANES * wide
    line = lax.broadcasted_iota(jnp.int32, (LANES, span), 0)
    column = lax.broadcasted_iota(jnp.int32, (LANES, span), 1)
    stretch = jnp.where((column >= line * wide) & (column < line * wide + wide), 1.0, 0.0).astype(jnp.bfloat16)
    for h in range(coarse // LANES):
        flags = refine[:, h * LANES : (h + 1) * LANES].astype(jnp.float32).astype(jnp.bfloat16)
        grown = jnp.dot(flags, stretch, preferred_element_type=jnp.float32)
        for i in range(wide):
            marks[h * wide + i] = grown[:, i * LANES : (i + 1) * LANES]

    pieces = plane_s.shape[1]
    band = rows // pieces
    has_next, has_prior = los < los_count - 1, los > 0

    def beside(i, p):
        at = pl.ds(p * band, band)
        return pltpu.make_async_remote_copy(
            src_ref=density.at[slab - 1 if i == 0 else 0, at, :],
            dst_ref=(below if i == 0 else above).at[at, :],
            send_sem=plane_s.at[i, p], recv_sem=plane_r.at[i, p],
            device_id={"los": lax.rem(los + (1 if i == 0 else los_count - 1), los_count)}, device_id_type=mesh,
        )

    outside_in = [0, pieces - 1] + list(range(1, pieces - 1))
    pl.semaphore_wait(barrier, sky_count + los_count - 2)
    for p in outside_in:
        pl.when(has_next)(beside(0, p).start)
        pl.when(has_prior)(beside(1, p).start)

    def fill(r, carry):
        load(r).wait()
        start = pl.multiple_of(r * deep, deep)
        into = pl.ds(pl.multiple_of(start + SUB, SUB), deep)
        for z in range(slab):
            for t in range(tiles):
                cells[z, t, into, :] = raw[z, pl.ds(start, deep), t * LANES : (t + 1) * LANES].astype(jnp.float32)
        return carry

    lax.fori_loop(0, 2, lambda i, carry: fill(i * (strips - 1), carry), 0)

    def hop(source, target, i, axis, me, count, shift):
        return pltpu.make_async_remote_copy(
            src_ref=source, dst_ref=target, send_sem=halo_s.at[i], recv_sem=halo_r.at[i],
            device_id={axis: lax.rem(me + shift, count)}, device_id_type=mesh,
        )

    def rim(ref, i, lead):
        both = []
        for source, target, shift in ((SUB + rows - 1, SUB - 1, 1), (SUB, SUB + rows, sky_count - 1)):
            index = (slice(None),) * lead
            both.append(
                hop(
                    ref.at[index + (pl.ds(source, 1),)], ref.at[index + (pl.ds(target, 1),)],
                    i + len(both), "sky", sky, sky_count, shift,
                )
            )
        return both

    sides = rim(cells, 0, 2)
    for copy in sides:
        copy.start()
    for fetch in fetches[3:]:
        fetch.start()

    lane8 = lax.broadcasted_iota(jnp.int32, (SUB, LANES), 1)
    lane_first, lane_last = lane8 == 0, lane8 == LANES - 1

    def chunk(r, carry):
        start = pl.multiple_of(r * SUB, SUB)
        at = pl.multiple_of(start + SUB, SUB)
        here, up, down = pl.ds(at, SUB), pl.ds(at - 1, SUB), pl.ds(at + 1, SUB)
        batch = 4
        for first in range(0, tiles, batch):
            ours = range(first, first + batch)
            total = [[None] * batch for _ in range(4)]

            def put(i, w, value):
                total[i][w] = value if total[i][w] is None else total[i][w] + value

            mid = [cells[0, t, here, :] for t in ours]
            step_z = [None] * batch
            for z in range(slab):
                prior = cells[z, (first - 1) % tiles, here, :]
                later = cells[z, (first + batch) % tiles, here, :]
                left = [pltpu.roll(v, LANES - 1, 1) for v in mid + [later]]
                right = [pltpu.roll(v, 1, 1) for v in [prior] + mid]
                for w, t in enumerate(ours):
                    v = mid[w]
                    put(0, w, average[z] * v)
                    put(2, w, average[z] * median0(cells[z, t, down, :] - v, v - cells[z, t, up, :]))
                    ahead = jnp.where(lane_last, left[w + 1], left[w])
                    behind = jnp.where(lane_first, right[w], right[w + 1])
                    put(3, w, average[z] * median0(ahead - v, v - behind))
                    if z < slab - 1:
                        above_v = cells[z + 1, t, here, :]
                        next_z = above_v - v
                        if z > 0:
                            put(1, w, slope[z] * median0(next_z, step_z[w]))
                        mid[w], step_z[w] = above_v, next_z
            for i in range(4):
                for w, t in enumerate(ours):
                    value = total[i][w]
                    sums[i, t, pl.ds(start, SUB), :] = jnp.zeros((SUB, LANES), jnp.float32) if value is None else value
        return carry

    def sweep(b, carry):
        fill(b + 1, carry)
        return lax.fori_loop(2 * b + 1, 2 * b + 3, chunk, carry)

    lax.fori_loop(0, strips - 2, sweep, 0)
    lax.fori_loop(2 * strips - 3, 2 * strips - 1, chunk, 0)
    for copy in sides:
        copy.wait()
    lax.fori_loop(0, 2, lambda i, carry: chunk(i * (rows // SUB - 1), carry), 0)

    def edge(p, z, inner, outer, sign):
        def add_edge(r, carry):
            start = pl.multiple_of(r * deep, deep)
            at = pl.ds(pl.multiple_of(start + SUB, SUB), deep)
            here = pl.ds(start, deep)
            for t in range(tiles):
                v = cells[z, t, at, :]
                u = outer[here, t * LANES : (t + 1) * LANES].astype(jnp.float32)
                sums[1, t, here, :] += (sign * slope[z]) * median0(cells[inner, t, at, :] - v, v - u)
            return carry

        lax.fori_loop(p * band // deep, (p + 1) * band // deep, add_edge, 0)

    def late(r, carry):
        start = pl.multiple_of(r * SUB, SUB)
        here = pl.ds(start, SUB)
        into = pl.ds(pl.multiple_of(start + SUB, SUB), SUB)
        known = {}

        def item(t):
            if t not in known:
                mark = marks[t, pl.ds(r, 1), :]
                base = sums[0, t, here, :]
                refined = mark * base
                rest[t, here, :] = base - refined
                f = refined + mark * sums[1, t, here, :]
                slant = mark * sums[3, t, here, :] * (1.0 / 32.0)
                g = mark * sums[2, t, here, :]
                e = 0.125 * f
                known[t] = (
                    f, g, pltpu.roll(e + slant, 1, 1), pltpu.roll(e - slant, LANES - 1, 1),
                    pltpu.roll(g, 1, 1), pltpu.roll(g, LANES - 1, 1),
                )
            return known[t]

        for t in range(tiles):
            one, two, three = item((t - 1) % tiles), item(t), item((t + 1) % tiles)
            smooth[t, into, :] = (
                0.75 * two[0] + jnp.where(lane_first, one[2], two[2]) + jnp.where(lane_last, three[3], two[3])
            )
            tilt[t, into, :] = 0.75 * two[1] + 0.125 * (
                jnp.where(lane_first, one[4], two[4]) + jnp.where(lane_last, three[5], two[5])
            )
        return carry

    def finish(r, carry):
        start = pl.multiple_of(r * SUB, SUB)
        at = pl.multiple_of(start + SUB, SUB)
        here, up, down = pl.ds(at, SUB), pl.ds(at - 1, SUB), pl.ds(at + 1, SUB)
        into = pl.ds(start, SUB)
        parts = []
        for t in range(tiles):
            deposit = (
                rest[t, into, :]
                + 0.75 * smooth[t, here, :]
                + 0.125 * (smooth[t, up, :] + smooth[t, down, :])
                + (tilt[t, up, :] - tilt[t, down, :]) * (1.0 / 32.0)
            )
            parts.append((deposit, None))
        modes = fft_list(parts, -1.0)
        for c in range(tiles // 2):
            two = (modes[0][0], modes[tiles // 2][0]) if c == 0 else modes[c]
            relative = lax.rem(c // groups - los + los_count, los_count)
            for j in range(2):
                fold[relative, c % groups, j, into, :] = two[j]
        return carry

    middle = 2 * band // SUB - 1
    rims = rim(smooth, 2, 1) + rim(tilt, 4, 1)
    for done, p in enumerate(outside_in):

        @pl.when(has_prior)
        def _():
            beside(0, p).wait_recv()
            edge(p, 0, 1, below, 1.0)

        @pl.when(has_next)
        def _():
            beside(1, p).wait_recv()
            edge(p, slab - 1, slab - 2, above, -1.0)

        lax.fori_loop(p * band // SUB, (p + 1) * band // SUB, late, 0)
        if done == 1:
            for copy in rims:
                copy.start()
        if done == 2:
            lax.fori_loop(1, middle, finish, 0)

    lax.fori_loop(middle, rows // SUB - 1, finish, 0)
    for copy in rims:
        copy.wait()
    lax.fori_loop(0, 2, lambda i, carry: finish(i * (rows // SUB - 1), carry), 0)

    def share(g, i):
        return pltpu.make_async_remote_copy(
            src_ref=hop_send.at[i - 1, g], dst_ref=hop_recv.at[los_count - 1 - i, g],
            send_sem=hs.at[i, g], recv_sem=hr.at[i, g],
            device_id={"los": lax.rem(los + i, los_count)}, device_id_type=mesh,
        )

    for g in range(groups):
        for i in range(1, los_count):
            re, im = fold[i, g, 0], fold[i, g, 1]
            if g == 0:
                words, level, wide = pack(re, im, re[0:1], True)
                hop_send[i - 1, g, rows + 1 : rows + 2, :] = wide
            else:
                words, level, _ = pack(re, im)
            hop_send[i - 1, g, 0:rows, :] = words
            hop_send[i - 1, g, rows : rows + 1, :] = level
            share(g, i).start()

    pair = 2
    part = LANES // sky_count
    each = groups // chunks
    count = each * part
    classes = length // LANES // 2
    half = LANES // 2

    def mode_of(kind, j):
        n = jnp.where(kind == 0, jnp.where(j < half, tiles * j, tiles * (j - half) + classes), kind + tiles * j)
        return jnp.where(n >= length // 2, n - length, n)

    near = [d for i in range(1, sky_count // 2) for d in (i, sky_count - i)] + [sky_count // 2]
    shifts = [d for two in zip(near[::-1], near) for d in two][: sky_count - 1]

    def sky_copy(source, target, send, recv, i):
        peer = lax.rem(sky + i, sky_count)
        return pltpu.make_async_remote_copy(
            src_ref=source(peer), dst_ref=target, send_sem=send, recv_sem=recv,
            device_id={"sky": peer}, device_id_type=mesh,
        )

    def forward_copy(c, i):
        size = count + (2 if c == 0 else 1)
        return sky_copy(
            lambda peer: fsend.at[c, peer, pl.ds(0, size)], frecv.at[c, sky, pl.ds(0, size)],
            fs.at[c], fr.at[c], i,
        )

    def backward_copy(f, c, i):
        return sky_copy(
            lambda peer: bsend.at[f, c, peer, pl.ds(0, count + 1)], brecv.at[f, c, sky, pl.ds(0, count + 1)],
            bs.at[f, c], br.at[f, c], i,
        )

    def drain(ref, size, semaphore):
        part_of = ref.at[pl.ds(0, sky_count - 1), pl.ds(0, size)]
        pltpu.make_async_copy(part_of, part_of, semaphore).wait()

    def cross_copy(f, c, i):
        return pltpu.make_async_remote_copy(
            src_ref=brecv.at[f, c, :, pl.ds(0, count + 1)],
            dst_ref=cross.at[los_count - 1 - i, f, c, :, pl.ds(0, count + 1)],
            send_sem=xs.at[f, c, i], recv_sem=xr.at[f, c, i],
            device_id={"los": lax.rem(los + i, los_count)}, device_id_type=mesh,
        )

    unit = 2.0 * math.pi / length
    base = -2.0 / (unit * float(length) * float(length) * float(layers))

    def masks(c, shape):
        line = lax.broadcasted_iota(jnp.int32, shape, 0)
        packed = (line == 0) & (los == 0) & (sky == 0) if c == 0 else None
        return line, packed

    for c in range(chunks):
        extra = SUB if c == 0 else 0
        total = count + extra
        line, packed = masks(c, (total, rows))
        lane = lax.broadcasted_iota(jnp.int32, (total, rows), 1)
        n = mode_of(los * groups + c * each + line // part, sky * part + line % part)
        single = line >= count
        if c == 0:
            n = jnp.where(single, length // 2, n)
            single = single | packed
        ny = n.astype(jnp.float32)
        odd_y = jnp.where(n == length // 2, 0.0, ny)
        weight = jnp.where(single, base, 2.0 * base) * jnp.sqrt(jnp.maximum(jnp.abs(ny), 1.0))
        for k in range(sky_count):
            nx = k + sky_count * lane
            nx = jnp.where(nx >= length // 2, nx - length, nx)
            odd_x = jnp.where(nx == -(length // 2), 0, nx).astype(jnp.float32)
            square = nx.astype(jnp.float32) * nx.astype(jnp.float32) + ny * ny
            factor = jnp.where(square == 0.0, 0.0, weight / jnp.where(square == 0.0, 1.0, square))
            scales[c, 0, k, 0:total, :] = odd_x * factor
            scales[c, 1, k, 0:total, :] = odd_y * factor

    order = lax.broadcasted_iota(jnp.int32, (LANES, rows), 0)
    for fetch in fetches[3:]:
        fetch.wait()
    for c in range(chunks):
        for g in range(c * each, (c + 1) * each):
            sides = [fold[0, g, j] for j in range(pair)]
            for i in range(1, los_count):
                share(g, i).wait_recv()
                slot = los_count - 1 - i
                re, im, step = unpack(hop_recv[slot, g, 0:rows, :], hop_recv[slot, g, rows : rows + 1, :])
                if g == 0:
                    re = re + hop_recv[slot, g, rows + 1 : rows + 2, :].astype(jnp.float32) * step
                sides = [sides[0] + re, sides[1] + im]
            kind = los * groups + g
            z = dot(table[kind], jnp.concatenate(sides, axis=1), ((1,), (1,)))
            n = jnp.maximum(jnp.abs(mode_of(kind, order)), 1).astype(jnp.float32)
            weight = lax.rsqrt(n)
            nyquist = (kind == 0) & (order == 0)
            spectra[g, 0] = z[:LANES] * weight
            spectra[g, 1] = z[LANES:] * jnp.where(nyquist, 1.0 / math.sqrt(length // 2), weight)
        for d in range(sky_count):
            re, im = [
                jnp.concatenate(
                    [spectra[g, j, d * part : (d + 1) * part, :] for g in range(c * each, (c + 1) * each)], axis=0
                )
                for j in range(pair)
            ]
            spare = None
            if c == 0:
                spare = re[0:1]
                re = jnp.where(lax.broadcasted_iota(jnp.int32, re.shape, 0) == 0, 0.0, re)
            words, level, wide = pack(re, im, spare)
            fsend[c, d, 0:count, :] = words
            fsend[c, d, count : count + 1, :] = level
            if c == 0:
                fsend[c, d, count + 1 : count + 2, :] = wide
        for i in shifts:
            forward_copy(c, i).start()
        frecv[c, pl.ds(sky, 1)] = fsend[c, pl.ds(sky, 1)]

    def relay(f, c):
        drain(brecv.at[f, c], count + 1, br.at[f, c])
        for i in range(1, los_count):
            cross_copy(f, c, i).start()

    for c in range(chunks):
        extra = SUB if c == 0 else 0
        total = count + extra
        line, packed = masks(c, (total, rows))
        drain(frecv.at[c], count + (2 if c == 0 else 1), fr.at[c])
        items = []
        for s in range(sky_count):
            re, im, step = unpack(frecv[c, s, 0:count, :], frecv[c, s, count : count + 1, :])
            if c == 0:
                wide = frecv[c, s, count + 1 : count + 2, :].astype(jnp.float32) * step
                re = jnp.where(line[:count] == 0, wide, re)
                zero = jnp.zeros((extra, rows), jnp.float32)
                re = jnp.concatenate([re, jnp.broadcast_to(im[0:1], (extra, rows))], axis=0)
                im = jnp.where(packed, 0.0, jnp.concatenate([im, zero], axis=0))
            items.append((re, im))
        items = fft_list(items, -1.0)
        turned = []
        for k, (re, im) in enumerate(items):
            co, si = twist[k, 0:1, :], twist[k, 1:2, :]
            turned.append(jnp.concatenate([re * co + im * si, im * co - re * si], axis=1))
        spectrum = dot(jnp.concatenate(turned, axis=0), forward[...], ((1,), (0,)))
        for f in range(2):
            fields = []
            for k in range(sky_count):
                here = spectrum[k * total : (k + 1) * total]
                scale = scales[c, f, k, 0:total, :]
                fields.append(jnp.concatenate([-scale * here[:, rows:], scale * here[:, :rows]], axis=1))
            values = dot(jnp.concatenate(fields, axis=0), forward[...], ((1,), (1,)))
            items = []
            for k in range(sky_count):
                here = values[k * total : (k + 1) * total]
                re, im = here[:, :rows], here[:, rows:]
                co, si = twist[k, 0:1, :], twist[k, 1:2, :]
                items.append((re * co - im * si, im * co + re * si))
            items = fft_list(items, 1.0)
            for s in range(sky_count):
                re, im = items[s]
                if c == 0:
                    im = jnp.where(packed[:count], jnp.broadcast_to(re[count : count + 1], (count, rows)), im[:count])
                    re = re[:count]
                words, level, _ = pack(re, im)
                bsend[f, c, s, 0:count, :] = words
                bsend[f, c, s, count : count + 1, :] = level
            for i in shifts:
                backward_copy(f, c, i).start()
            brecv[f, c, pl.ds(sky, 1)] = bsend[f, c, pl.ds(sky, 1)]
            if c:
                relay(f, c - 1)

    inner = out_x.shape[1] // LANES
    fresh = [True, True]

    def plane(f, c, block, owner):
        parts = [unpack(block[s, 0:count, :], block[s, count : count + 1, :]) for s in range(sky_count)]
        pieces = []
        for g in range(each):
            z = jnp.concatenate([p[j][g * part : (g + 1) * part] for j in range(pair) for p in parts], axis=0)
            kind = owner * groups + c * each + g
            both = dot(z, table[kind], ((0,), (0,)))
            pieces.append((kind, both[:, :LANES], both[:, LANES:]))
        for i in range(inner):
            tile = slice(i * LANES, (i + 1) * LANES)
            total = None if fresh[f] else outs[f][:, tile]
            for kind, one, two in pieces:
                at = 2 * (kind * tiles + los * inner + i)
                term = mix[at] * one + mix[at + 1] * two
                total = term if total is None else total + term
            outs[f][:, tile] = total
        fresh[f] = False


    def collect(f, c):
        for i in range(1, los_count):
            cross_copy(f, c, i).wait_recv()
            slot = los_count - 1 - i
            plane(f, c, cross.at[slot, f, c], lax.rem(los + los_count - i, los_count))

    def own(f, c):
        plane(f, c, brecv.at[f, c], los)

    end = chunks - 1
    for c in range(end):
        own(0, c)
        own(1, c)
        collect(0, c)
        if c == end - 1:
            relay(0, end)
        collect(1, c)
    if not end:
        relay(0, end)
    relay(1, end)
    own(0, end)
    own(1, end)
    collect(0, end)
    collect(1, end)
    for p in range(pieces):
        pl.when(has_next)(beside(0, p).wait_send)
        pl.when(has_prior)(beside(1, p).wait_send)
    for g in range(groups):
        for i in range(1, los_count):
            share(g, i).wait_send()
    for c in range(chunks):
        drain(fsend.at[c], count + (2 if c == 0 else 1), fs.at[c])
        for f in range(2):
            drain(bsend.at[f, c], count + 1, bs.at[f, c])
        for f in range(2):
            for i in range(1, los_count):
                cross_copy(f, c, i).wait_send()


def emit_kernel(x_in, y_in, x_out, y_out, done):
    copies = [
        pltpu.make_async_copy(source, target, done.at[i])
        for i, (source, target) in enumerate(((x_in, x_out), (y_in, y_out)))
    ]
    for copy in copies:
        copy.start()
    for copy in copies:
        copy.wait()


def body(density, refine, weight_low, weight_high):
    los_count, sky_count = lax.axis_size("los"), lax.axis_size("sky")
    slab, rows, width = density.shape
    length = rows * sky_count
    tiles = width // LANES
    groups = tiles // 2 // los_count
    part = LANES // sky_count
    table = row_table(width)
    forward, twist = column_tables(length, sky_count)
    mix = tile_table(width).reshape(-1)
    chunks = next(n for n in (4, 2, 1) if groups % n == 0)
    peers = (sky_count, -(-(groups // chunks * part + 2) // SUB) * SUB, rows)
    scaled = (sky_count, groups // chunks * part + SUB, rows)
    operands = (density, refine[0], weight_low, weight_high, table, forward, twist, mix)
    dma = pltpu.SemaphoreType.DMA
    f32, i32 = jnp.float32, jnp.int32
    planes = pl.pallas_call(
        functools.partial(lens_kernel, length, los_count, sky_count, groups, chunks),
        out_shape=(jax.ShapeDtypeStruct((rows, width // los_count), f32),) * 2,
        in_specs=[HBM] * 8,
        out_specs=(VMEM, VMEM),
        scratch_shapes=[
            pltpu.VMEM((slab, rows, width), density.dtype),
            pltpu.VMEM((slab, tiles, rows + 2 * SUB, LANES), f32),
            pltpu.VMEM((rows, width), density.dtype),
            pltpu.VMEM((rows, width), density.dtype),
            pltpu.VMEM((tiles, refine.shape[1], LANES), f32),
            pltpu.VMEM((4, tiles, rows, LANES), f32),
            pltpu.VMEM((tiles, rows, LANES), f32),
            pltpu.VMEM((tiles, rows + 2 * SUB, LANES), f32),
            pltpu.VMEM((tiles, rows + 2 * SUB, LANES), f32),
            pltpu.VMEM((los_count, groups, 2, rows, LANES), f32),
            pltpu.VMEM((los_count - 1, groups, rows + SUB, LANES), i32),
            pltpu.VMEM((los_count - 1, groups, rows + SUB, LANES), i32),
            pltpu.VMEM(table.shape, f32),
            pltpu.VMEM(forward.shape, f32),
            pltpu.VMEM(twist.shape, f32),
            pltpu.VMEM(refine.shape[1:], i32),
            pltpu.SMEM((slab,), f32),
            pltpu.SMEM((slab,), f32),
            pltpu.SMEM(mix.shape, f32),
            pltpu.VMEM((groups, 2, LANES, rows), f32),
            pltpu.VMEM((chunks,) + peers, i32),
            pltpu.VMEM((chunks,) + peers, i32),
            pltpu.VMEM((2, chunks) + peers, i32),
            pltpu.VMEM((2, chunks) + peers, i32),
            pltpu.VMEM((los_count - 1, 2, chunks) + peers, i32),
            pltpu.VMEM((chunks, 2) + scaled, f32),
            dma((7,)),
            dma((rows // 16,)),
            dma((2, 4)),
            dma((2, 4)),
            dma((6,)),
            dma((6,)),
            dma((los_count, groups)),
            dma((los_count, groups)),
            dma((chunks,)),
            dma((chunks,)),
            dma((2, chunks)),
            dma((2, chunks)),
            dma((2, chunks, los_count)),
            dma((2, chunks, los_count)),
        ],
        compiler_params=pltpu.CompilerParams(
            vmem_limit_bytes=48 * 1024 * 1024, collective_id=0, has_side_effects=True
        ),
    )(*[pltpu.with_memory_space_constraint(x, pltpu.HBM) for x in operands])
    return pl.pallas_call(
        emit_kernel,
        out_shape=tuple(jax.ShapeDtypeStruct(plane.shape, f32) for plane in planes),
        in_specs=[ANY, ANY],
        out_specs=(HBM, HBM),
        scratch_shapes=[dma((2,))],
        compiler_params=pltpu.CompilerParams(vmem_limit_bytes=1024 * 1024),
    )(*planes)


def solution(mesh):
    placed = (P("los", "sky", None), P("los", "sky", None), P("los"), P("los"))
    return jax.shard_map(
        body,
        mesh=mesh,
        in_specs=placed,
        out_specs=(P("sky", "los"), P("sky", "los")),
        check_vma=False,
    )
```

```python
import functools
import math

import jax
import jax.numpy as jnp
import numpy as np
from jax import lax
from jax.experimental import pallas as pl
from jax.experimental.pallas import tpu as pltpu
from jax.sharding import PartitionSpec as P

LANES = 128
SUB = 8
VMEM = pl.BlockSpec(memory_space=pltpu.VMEM)
SMEM = pl.BlockSpec(memory_space=pltpu.SMEM)
ANY = pl.BlockSpec(memory_space=pl.ANY)
HBM = pl.BlockSpec(memory_space=pltpu.HBM)


def median0(a, b):
    return jnp.maximum(jnp.minimum(a, b), jnp.minimum(jnp.maximum(a, b), 0.0))


def add(p, q):
    im = q[1] if p[1] is None else (p[1] if q[1] is None else p[1] + q[1])
    return (p[0] + q[0], im)


def sub(p, q):
    if q[1] is None:
        return (p[0] - q[0], p[1])
    return (p[0] - q[0], -q[1] if p[1] is None else p[1] - q[1])


def turn(p, angle):
    c, s = math.cos(angle), math.sin(angle)
    re, im = p
    if abs(s) < 1e-12:
        return p if c > 0 else (-re, None if im is None else -im)
    if abs(c) < 1e-12:
        sign = 1.0 if s > 0 else -1.0
        if im is None:
            return (jnp.zeros_like(re), sign * re)
        return (-im, re) if s > 0 else (im, -re)
    if im is None:
        return (c * re, s * re)
    return (c * re - s * im, s * re + c * im)


def fft_list(items, flip):
    count = len(items)
    if count == 1:
        return items
    even = fft_list(items[0::2], flip)
    odd = fft_list(items[1::2], flip)
    first, second = [], []
    for k in range(count // 2):
        w = turn(odd[k], flip * 2.0 * math.pi * k / count)
        first.append(add(even[k], w))
        second.append(sub(even[k], w))
    return first + second


def row_table(width):
    tiles = width // LANES
    classes = tiles // 2
    half = LANES // 2
    t = np.arange(LANES)
    table = np.zeros((classes, 2 * LANES, 2 * LANES))

    def angles(n):
        return 2.0 * np.pi * ((n[:, None] * t[None, :]) % width) / width

    for c in range(classes):
        if c == 0:
            j = np.arange(half)
            low = angles(tiles * j)
            high = angles(tiles * j + classes)
            table[0, :half, :LANES] = np.cos(low)
            table[0, half:LANES, LANES:] = np.cos(high)
            table[0, LANES : LANES + half, :LANES] = -np.sin(low)
            table[0, LANES, :LANES] = np.cos(np.pi * t)
            table[0, LANES + half :, LANES:] = -np.sin(high)
        else:
            a = angles(c + tiles * np.arange(LANES))
            table[c, :LANES, :LANES] = np.cos(a)
            table[c, :LANES, LANES:] = np.sin(a)
            table[c, LANES:, :LANES] = -np.sin(a)
            table[c, LANES:, LANES:] = np.cos(a)
    return jnp.asarray(table, jnp.float32)


def tile_table(width):
    tiles = width // LANES
    classes = tiles // 2
    s = np.arange(tiles)
    table = np.zeros((classes, 2 * tiles))
    for c in range(classes):
        if c == 0:
            table[c, 0::2] = 1.0
            table[c, 1::2] = np.where(s % 2 == 0, 1.0, -1.0)
        else:
            table[c, 0::2] = np.cos(2.0 * np.pi * s * c / tiles)
            table[c, 1::2] = -np.sin(2.0 * np.pi * s * c / tiles)
    return jnp.asarray(table, jnp.float32)


def column_tables(length, sky):
    rows = length // sky
    t = np.arange(rows)
    a = 2.0 * np.pi * (t[:, None] * t[None, :] % rows) / rows
    c, s = np.cos(a), np.sin(a)
    forward = np.block([[c, -s], [s, c]])
    b = 2.0 * np.pi * (np.arange(sky)[:, None] * t[None, :]) / length
    twist = np.stack([np.cos(b), np.sin(b)], axis=1)
    return jnp.asarray(forward, jnp.float32), jnp.asarray(twist, jnp.float32)


def dot(a, b, dims):
    return lax.dot_general(
        a, b, (dims, ((), ())), precision=lax.Precision.HIGHEST, preferred_element_type=jnp.float32
    )


def pack(re, im, spare=None, centred=False):
    size = jnp.max(jnp.maximum(jnp.abs(re - spare if centred else re), jnp.abs(im)), axis=0, keepdims=True)
    if spare is not None:
        size = jnp.maximum(size, jnp.abs(spare) * (1.0 / 16384.0))
    level = jnp.ceil(jnp.log2(jnp.maximum(size, 1e-30) * (1.0 / 32700.0)) * 32.0)
    inverse = jnp.exp2(level * (-1.0 / 32.0))
    wide = None if spare is None else jnp.floor(spare * inverse + 0.5).astype(jnp.int32)
    if centred:
        re = re - wide.astype(jnp.float32) * jnp.exp2(level * (1.0 / 32.0))
    high = (re * inverse + 32768.5).astype(jnp.int32)
    low = (im * inverse + 32768.5).astype(jnp.int32)
    words = lax.shift_left(high, jnp.full_like(high, 16)) | low
    return words, level.astype(jnp.int32), wide


def unpack(words, level):
    step = jnp.exp2(level.astype(jnp.float32) * (1.0 / 32.0))
    high = lax.shift_right_logical(words, jnp.full_like(words, 16)).astype(jnp.float32)
    low = (words & 65535).astype(jnp.float32)
    return (high - 32768.0) * step, (low - 32768.0) * step, step


def lens_kernel(length, los_count, sky_count, groups, chunks, *refs):
    (
        density, refine_in, low_in, high_in, table_in, forward_in, twist_in, mix_in, out_x, out_y,
        raw, cells, below, above, marks, sums, rest, smooth, tilt, fold, hop_send, hop_recv,
        table, forward, twist, refine, weight_low, weight_high, mix, spectra, fsend, frecv, bsend, brecv, cross, scales, local,
        loads, plane_s, plane_r, halo_s, halo_r, hs, hr, fs, fr, bs, br, xs, xr,
    ) = refs
    outs = (out_x, out_y)
    mesh = pl.DeviceIdType.MESH
    los, sky = lax.axis_index("los"), lax.axis_index("sky")
    barrier = pltpu.get_barrier_semaphore()
    for i in range(1, sky_count):
        pl.semaphore_signal(barrier, inc=1, device_id={"sky": lax.rem(sky + i, sky_count)}, device_id_type=mesh)
    for i in range(1, los_count):
        pl.semaphore_signal(barrier, inc=1, device_id={"los": lax.rem(los + i, los_count)}, device_id_type=mesh)
    slab, rows, width = density.shape
    layers = slab * los_count
    tiles = width // LANES
    deep = 16

    def load(r):
        at = pl.ds(pl.multiple_of(r * deep, deep), deep)
        return pltpu.make_async_copy(density.at[:, at, :], raw.at[:, at, :], loads.at[r])

    strips = rows // deep
    for r in [0, strips - 1] + list(range(1, strips - 1)):
        load(r).start()
    fetches = [
        pltpu.make_async_copy(source, target, local.at[i])
        for i, (source, target) in enumerate(
            (
                (refine_in, refine), (low_in, weight_low), (high_in, weight_high),
                (table_in, table), (forward_in, forward), (twist_in, twist), (mix_in, mix),
            )
        )
    ]
    for fetch in fetches[:3]:
        fetch.start()

    for fetch in fetches[:3]:
        fetch.wait()
    average = [0.5 * (weight_low[z] + weight_high[z]) for z in range(slab)]
    slope = [0.125 * (weight_high[z] - weight_low[z]) for z in range(slab)]
    blocks, coarse = refine.shape
    wide = width // coarse
    span = LANES * wide
    line = lax.broadcasted_iota(jnp.int32, (LANES, span), 0)
    column = lax.broadcasted_iota(jnp.int32, (LANES, span), 1)
    stretch = jnp.where((column >= line * wide) & (column < line * wide + wide), 1.0, 0.0).astype(jnp.bfloat16)
    for h in range(coarse // LANES):
        flags = refine[:, h * LANES : (h + 1) * LANES].astype(jnp.float32).astype(jnp.bfloat16)
        grown = jnp.dot(flags, stretch, preferred_element_type=jnp.float32)
        for i in range(wide):
            marks[h * wide + i] = grown[:, i * LANES : (i + 1) * LANES]

    pieces = plane_s.shape[1]
    band = rows // pieces
    has_next, has_prior = los < los_count - 1, los > 0

    def beside(i, p):
        at = pl.ds(p * band, band)
        return pltpu.make_async_remote_copy(
            src_ref=density.at[slab - 1 if i == 0 else 0, at, :],
            dst_ref=(below if i == 0 else above).at[at, :],
            send_sem=plane_s.at[i, p], recv_sem=plane_r.at[i, p],
            device_id={"los": lax.rem(los + (1 if i == 0 else los_count - 1), los_count)}, device_id_type=mesh,
        )

    outside_in = [0, pieces - 1] + list(range(1, pieces - 1))
    pl.semaphore_wait(barrier, sky_count + los_count - 2)
    for p in outside_in:
        pl.when(has_next)(beside(0, p).start)
        pl.when(has_prior)(beside(1, p).start)

    def fill(r, carry):
        load(r).wait()
        start = pl.multiple_of(r * deep, deep)
        into = pl.ds(pl.multiple_of(start + SUB, SUB), deep)
        for z in range(slab):
            for t in range(tiles):
                cells[z, t, into, :] = raw[z, pl.ds(start, deep), t * LANES : (t + 1) * LANES].astype(jnp.float32)
        return carry

    lax.fori_loop(0, 2, lambda i, carry: fill(i * (strips - 1), carry), 0)

    def hop(source, target, i, axis, me, count, shift):
        return pltpu.make_async_remote_copy(
            src_ref=source, dst_ref=target, send_sem=halo_s.at[i], recv_sem=halo_r.at[i],
            device_id={axis: lax.rem(me + shift, count)}, device_id_type=mesh,
        )

    def rim(ref, i, lead):
        both = []
        for source, target, shift in ((SUB + rows - 1, SUB - 1, 1), (SUB, SUB + rows, sky_count - 1)):
            index = (slice(None),) * lead
            both.append(
                hop(
                    ref.at[index + (pl.ds(source, 1),)], ref.at[index + (pl.ds(target, 1),)],
                    i + len(both), "sky", sky, sky_count, shift,
                )
            )
        return both

    sides = rim(cells, 0, 2)
    for copy in sides:
        copy.start()
    for fetch in fetches[3:]:
        fetch.start()

    lane8 = lax.broadcasted_iota(jnp.int32, (SUB, LANES), 1)
    lane_first, lane_last = lane8 == 0, lane8 == LANES - 1

    def chunk(r, carry):
        start = pl.multiple_of(r * SUB, SUB)
        at = pl.multiple_of(start + SUB, SUB)
        here, up, down = pl.ds(at, SUB), pl.ds(at - 1, SUB), pl.ds(at + 1, SUB)
        batch = 4
        for first in range(0, tiles, batch):
            ours = range(first, first + batch)
            total = [[None] * batch for _ in range(4)]

            def put(i, w, value):
                total[i][w] = value if total[i][w] is None else total[i][w] + value

            mid = [cells[0, t, here, :] for t in ours]
            step_z = [None] * batch
            for z in range(slab):
                prior = cells[z, (first - 1) % tiles, here, :]
                later = cells[z, (first + batch) % tiles, here, :]
                left = [pltpu.roll(v, LANES - 1, 1) for v in mid + [later]]
                right = [pltpu.roll(v, 1, 1) for v in [prior] + mid]
                for w, t in enumerate(ours):
                    v = mid[w]
                    put(0, w, average[z] * v)
                    put(2, w, average[z] * median0(cells[z, t, down, :] - v, v - cells[z, t, up, :]))
                    ahead = jnp.where(lane_last, left[w + 1], left[w])
                    behind = jnp.where(lane_first, right[w], right[w + 1])
                    put(3, w, average[z] * median0(ahead - v, v - behind))
                    if z < slab - 1:
                        above_v = cells[z + 1, t, here, :]
                        next_z = above_v - v
                        if z > 0:
                            put(1, w, slope[z] * median0(next_z, step_z[w]))
                        mid[w], step_z[w] = above_v, next_z
            for i in range(4):
                for w, t in enumerate(ours):
                    value = total[i][w]
                    sums[i, t, pl.ds(start, SUB), :] = jnp.zeros((SUB, LANES), jnp.float32) if value is None else value
        return carry

    def sweep(b, carry):
        fill(b + 1, carry)
        return lax.fori_loop(2 * b + 1, 2 * b + 3, chunk, carry)

    lax.fori_loop(0, strips - 2, sweep, 0)
    lax.fori_loop(2 * strips - 3, 2 * strips - 1, chunk, 0)
    for copy in sides:
        copy.wait()
    lax.fori_loop(0, 2, lambda i, carry: chunk(i * (rows // SUB - 1), carry), 0)

    def edge(p, z, inner, outer, sign):
        def add_edge(r, carry):
            start = pl.multiple_of(r * deep, deep)
            at = pl.ds(pl.multiple_of(start + SUB, SUB), deep)
            here = pl.ds(start, deep)
            for t in range(tiles):
                v = cells[z, t, at, :]
                u = outer[here, t * LANES : (t + 1) * LANES].astype(jnp.float32)
                sums[1, t, here, :] += (sign * slope[z]) * median0(cells[inner, t, at, :] - v, v - u)
            return carry

        lax.fori_loop(p * band // deep, (p + 1) * band // deep, add_edge, 0)

    def late(r, carry):
        start = pl.multiple_of(r * SUB, SUB)
        here = pl.ds(start, SUB)
        into = pl.ds(pl.multiple_of(start + SUB, SUB), SUB)
        known = {}

        def item(t):
            if t not in known:
                mark = marks[t, pl.ds(r, 1), :]
                base = sums[0, t, here, :]
                refined = mark * base
                rest[t, here, :] = base - refined
                f = refined + mark * sums[1, t, here, :]
                slant = mark * sums[3, t, here, :] * (1.0 / 32.0)
                g = mark * sums[2, t, here, :]
                e = 0.125 * f
                known[t] = (
                    f, g, pltpu.roll(e + slant, 1, 1), pltpu.roll(e - slant, LANES - 1, 1),
                    pltpu.roll(g, 1, 1), pltpu.roll(g, LANES - 1, 1),
                )
            return known[t]

        for t in range(tiles):
            one, two, three = item((t - 1) % tiles), item(t), item((t + 1) % tiles)
            smooth[t, into, :] = (
                0.75 * two[0] + jnp.where(lane_first, one[2], two[2]) + jnp.where(lane_last, three[3], two[3])
            )
            tilt[t, into, :] = 0.75 * two[1] + 0.125 * (
                jnp.where(lane_first, one[4], two[4]) + jnp.where(lane_last, three[5], two[5])
            )
        return carry

    def finish(r, carry):
        start = pl.multiple_of(r * SUB, SUB)
        at = pl.multiple_of(start + SUB, SUB)
        here, up, down = pl.ds(at, SUB), pl.ds(at - 1, SUB), pl.ds(at + 1, SUB)
        into = pl.ds(start, SUB)
        parts = []
        for t in range(tiles):
            deposit = (
                rest[t, into, :]
                + 0.75 * smooth[t, here, :]
                + 0.125 * (smooth[t, up, :] + smooth[t, down, :])
                + (tilt[t, up, :] - tilt[t, down, :]) * (1.0 / 32.0)
            )
            parts.append((deposit, None))
        modes = fft_list(parts, -1.0)
        for c in range(tiles // 2):
            two = (modes[0][0], modes[tiles // 2][0]) if c == 0 else modes[c]
            relative = lax.rem(c // groups - los + los_count, los_count)
            for j in range(2):
                fold[relative, c % groups, j, into, :] = two[j]
        return carry

    middle = 2 * band // SUB - 1
    rims = rim(smooth, 2, 1) + rim(tilt, 4, 1)
    for done, p in enumerate(outside_in):

        @pl.when(has_prior)
        def _():
            beside(0, p).wait_recv()
            edge(p, 0, 1, below, 1.0)

        @pl.when(has_next)
        def _():
            beside(1, p).wait_recv()
            edge(p, slab - 1, slab - 2, above, -1.0)

        lax.fori_loop(p * band // SUB, (p + 1) * band // SUB, late, 0)
        if done == 1:
            for copy in rims:
                copy.start()
        if done == 2:
            lax.fori_loop(1, middle, finish, 0)

    lax.fori_loop(middle, rows // SUB - 1, finish, 0)
    for copy in rims:
        copy.wait()
    lax.fori_loop(0, 2, lambda i, carry: finish(i * (rows // SUB - 1), carry), 0)

    def share(g, i):
        return pltpu.make_async_remote_copy(
            src_ref=hop_send.at[i - 1, g], dst_ref=hop_recv.at[los_count - 1 - i, g],
            send_sem=hs.at[i, g], recv_sem=hr.at[i, g],
            device_id={"los": lax.rem(los + i, los_count)}, device_id_type=mesh,
        )

    for g in range(groups):
        for i in range(1, los_count):
            re, im = fold[i, g, 0], fold[i, g, 1]
            if g == 0:
                words, level, wide = pack(re, im, re[0:1], True)
                hop_send[i - 1, g, rows + 1 : rows + 2, :] = wide
            else:
                words, level, _ = pack(re, im)
            hop_send[i - 1, g, 0:rows, :] = words
            hop_send[i - 1, g, rows : rows + 1, :] = level
            share(g, i).start()

    pair = 2
    part = LANES // sky_count
    each = groups // chunks
    count = each * part
    classes = length // LANES // 2
    half = LANES // 2

    def mode_of(kind, j):
        n = jnp.where(kind == 0, jnp.where(j < half, tiles * j, tiles * (j - half) + classes), kind + tiles * j)
        return jnp.where(n >= length // 2, n - length, n)

    near = [d for i in range(1, sky_count // 2) for d in (i, sky_count - i)] + [sky_count // 2]
    shifts = [d for two in zip(near[::-1], near) for d in two][: sky_count - 1]

    def sky_copy(source, target, send, recv, i):
        peer = lax.rem(sky + i, sky_count)
        return pltpu.make_async_remote_copy(
            src_ref=source(peer), dst_ref=target, send_sem=send, recv_sem=recv,
            device_id={"sky": peer}, device_id_type=mesh,
        )

    def forward_copy(c, i):
        size = count + (2 if c == 0 else 1)
        return sky_copy(
            lambda peer: fsend.at[c, peer, pl.ds(0, size)], frecv.at[c, sky, pl.ds(0, size)],
            fs.at[c], fr.at[c], i,
        )

    def backward_copy(f, c, i):
        return sky_copy(
            lambda peer: bsend.at[f, c, peer, pl.ds(0, count + 1)], brecv.at[f, c, sky, pl.ds(0, count + 1)],
            bs.at[f, c], br.at[f, c], i,
        )

    def drain(ref, size, semaphore):
        part_of = ref.at[pl.ds(0, sky_count - 1), pl.ds(0, size)]
        pltpu.make_async_copy(part_of, part_of, semaphore).wait()

    def cross_copy(f, c, i):
        return pltpu.make_async_remote_copy(
            src_ref=brecv.at[f, c, :, pl.ds(0, count + 1)],
            dst_ref=cross.at[los_count - 1 - i, f, c, :, pl.ds(0, count + 1)],
            send_sem=xs.at[f, c, i], recv_sem=xr.at[f, c, i],
            device_id={"los": lax.rem(los + i, los_count)}, device_id_type=mesh,
        )

    unit = 2.0 * math.pi / length
    base = -2.0 / (unit * float(length) * float(length) * float(layers))

    def masks(c, shape):
        line = lax.broadcasted_iota(jnp.int32, shape, 0)
        packed = (line == 0) & (los == 0) & (sky == 0) if c == 0 else None
        return line, packed

    for c in range(chunks):
        extra = SUB if c == 0 else 0
        total = count + extra
        line, packed = masks(c, (total, rows))
        lane = lax.broadcasted_iota(jnp.int32, (total, rows), 1)
        n = mode_of(los * groups + c * each + line // part, sky * part + line % part)
        single = line >= count
        if c == 0:
            n = jnp.where(single, length // 2, n)
            single = single | packed
        ny = n.astype(jnp.float32)
        odd_y = jnp.where(n == length // 2, 0.0, ny)
        weight = jnp.where(single, base, 2.0 * base) * jnp.sqrt(jnp.maximum(jnp.abs(ny), 1.0))
        for k in range(sky_count):
            nx = k + sky_count * lane
            nx = jnp.where(nx >= length // 2, nx - length, nx)
            odd_x = jnp.where(nx == -(length // 2), 0, nx).astype(jnp.float32)
            square = nx.astype(jnp.float32) * nx.astype(jnp.float32) + ny * ny
            factor = jnp.where(square == 0.0, 0.0, weight / jnp.where(square == 0.0, 1.0, square))
            scales[c, 0, k, 0:total, :] = odd_x * factor
            scales[c, 1, k, 0:total, :] = odd_y * factor

    order = lax.broadcasted_iota(jnp.int32, (LANES, rows), 0)
    for fetch in fetches[3:]:
        fetch.wait()
    for c in range(chunks):
        for g in range(c * each, (c + 1) * each):
            sides = [fold[0, g, j] for j in range(pair)]
            for i in range(1, los_count):
                share(g, i).wait_recv()
                slot = los_count - 1 - i
                re, im, step = unpack(hop_recv[slot, g, 0:rows, :], hop_recv[slot, g, rows : rows + 1, :])
                if g == 0:
                    re = re + hop_recv[slot, g, rows + 1 : rows + 2, :].astype(jnp.float32) * step
                sides = [sides[0] + re, sides[1] + im]
            kind = los * groups + g
            z = dot(table[kind], jnp.concatenate(sides, axis=1), ((1,), (1,)))
            n = jnp.maximum(jnp.abs(mode_of(kind, order)), 1).astype(jnp.float32)
            weight = lax.rsqrt(n)
            nyquist = (kind == 0) & (order == 0)
            spectra[g, 0] = z[:LANES] * weight
            spectra[g, 1] = z[LANES:] * jnp.where(nyquist, 1.0 / math.sqrt(length // 2), weight)
        for d in range(sky_count):
            re, im = [
                jnp.concatenate(
                    [spectra[g, j, d * part : (d + 1) * part, :] for g in range(c * each, (c + 1) * each)], axis=0
                )
                for j in range(pair)
            ]
            spare = None
            if c == 0:
                spare = re[0:1]
                re = jnp.where(lax.broadcasted_iota(jnp.int32, re.shape, 0) == 0, 0.0, re)
            words, level, wide = pack(re, im, spare)
            fsend[c, d, 0:count, :] = words
            fsend[c, d, count : count + 1, :] = level
            if c == 0:
                fsend[c, d, count + 1 : count + 2, :] = wide
        for i in shifts:
            forward_copy(c, i).start()
        frecv[c, pl.ds(sky, 1)] = fsend[c, pl.ds(sky, 1)]

    def relay(f, c):
        drain(brecv.at[f, c], count + 1, br.at[f, c])
        for i in range(1, los_count):
            cross_copy(f, c, i).start()

    for c in range(chunks):
        extra = SUB if c == 0 else 0
        total = count + extra
        line, packed = masks(c, (total, rows))
        drain(frecv.at[c], count + (2 if c == 0 else 1), fr.at[c])
        items = []
        for s in range(sky_count):
            re, im, step = unpack(frecv[c, s, 0:count, :], frecv[c, s, count : count + 1, :])
            if c == 0:
                wide = frecv[c, s, count + 1 : count + 2, :].astype(jnp.float32) * step
                re = jnp.where(line[:count] == 0, wide, re)
                zero = jnp.zeros((extra, rows), jnp.float32)
                re = jnp.concatenate([re, jnp.broadcast_to(im[0:1], (extra, rows))], axis=0)
                im = jnp.where(packed, 0.0, jnp.concatenate([im, zero], axis=0))
            items.append((re, im))
        items = fft_list(items, -1.0)
        turned = []
        for k, (re, im) in enumerate(items):
            co, si = twist[k, 0:1, :], twist[k, 1:2, :]
            turned.append(jnp.concatenate([re * co + im * si, im * co - re * si], axis=1))
        spectrum = dot(jnp.concatenate(turned, axis=0), forward[...], ((1,), (0,)))
        for f in range(2):
            fields = []
            for k in range(sky_count):
                here = spectrum[k * total : (k + 1) * total]
                scale = scales[c, f, k, 0:total, :]
                fields.append(jnp.concatenate([-scale * here[:, rows:], scale * here[:, :rows]], axis=1))
            values = dot(jnp.concatenate(fields, axis=0), forward[...], ((1,), (1,)))
            items = []
            for k in range(sky_count):
                here = values[k * total : (k + 1) * total]
                re, im = here[:, :rows], here[:, rows:]
                co, si = twist[k, 0:1, :], twist[k, 1:2, :]
                items.append((re * co - im * si, im * co + re * si))
            items = fft_list(items, 1.0)
            for s in range(sky_count):
                re, im = items[s]
                if c == 0:
                    im = jnp.where(packed[:count], jnp.broadcast_to(re[count : count + 1], (count, rows)), im[:count])
                    re = re[:count]
                words, level, _ = pack(re, im)
                bsend[f, c, s, 0:count, :] = words
                bsend[f, c, s, count : count + 1, :] = level
            for i in shifts:
                backward_copy(f, c, i).start()
            brecv[f, c, pl.ds(sky, 1)] = bsend[f, c, pl.ds(sky, 1)]
            if c:
                relay(f, c - 1)

    inner = out_x.shape[1] // LANES
    fresh = [True, True]

    def plane(f, c, block, owner):
        parts = [unpack(block[s, 0:count, :], block[s, count : count + 1, :]) for s in range(sky_count)]
        pieces = []
        for g in range(each):
            z = jnp.concatenate([p[j][g * part : (g + 1) * part] for j in range(pair) for p in parts], axis=0)
            kind = owner * groups + c * each + g
            both = dot(z, table[kind], ((0,), (0,)))
            pieces.append((kind, both[:, :LANES], both[:, LANES:]))
        for i in range(inner):
            tile = slice(i * LANES, (i + 1) * LANES)
            total = None if fresh[f] else outs[f][:, tile]
            for kind, one, two in pieces:
                at = 2 * (kind * tiles + los * inner + i)
                term = mix[at] * one + mix[at + 1] * two
                total = term if total is None else total + term
            outs[f][:, tile] = total
        fresh[f] = False


    def collect(f, c):
        for i in range(1, los_count):
            cross_copy(f, c, i).wait_recv()
            slot = los_count - 1 - i
            plane(f, c, cross.at[slot, f, c], lax.rem(los + los_count - i, los_count))

    def own(f, c):
        plane(f, c, brecv.at[f, c], los)

    end = chunks - 1
    early = [(f, c) for c in range(end) for f in range(2)]
    ready = [functools.partial(own, *step) for step in early] + [functools.partial(collect, *step) for step in early]
    first, second = 2 * end - 2, 3 * end - 1
    for step in ready[:first]:
        step()
    relay(0, end)
    for step in ready[first:second]:
        step()
    relay(1, end)
    own(0, end)
    own(1, end)
    for step in ready[second:]:
        step()
    collect(0, end)
    collect(1, end)
    for p in range(pieces):
        pl.when(has_next)(beside(0, p).wait_send)
        pl.when(has_prior)(beside(1, p).wait_send)
    for g in range(groups):
        for i in range(1, los_count):
            share(g, i).wait_send()
    for c in range(chunks):
        drain(fsend.at[c], count + (2 if c == 0 else 1), fs.at[c])
        for f in range(2):
            drain(bsend.at[f, c], count + 1, bs.at[f, c])
        for f in range(2):
            for i in range(1, los_count):
                cross_copy(f, c, i).wait_send()


def emit_kernel(x_in, y_in, x_out, y_out, done):
    copies = [
        pltpu.make_async_copy(source, target, done.at[i])
        for i, (source, target) in enumerate(((x_in, x_out), (y_in, y_out)))
    ]
    for copy in copies:
        copy.start()
    for copy in copies:
        copy.wait()


def body(density, refine, weight_low, weight_high):
    los_count, sky_count = lax.axis_size("los"), lax.axis_size("sky")
    slab, rows, width = density.shape
    length = rows * sky_count
    tiles = width // LANES
    groups = tiles // 2 // los_count
    part = LANES // sky_count
    table = row_table(width)
    forward, twist = column_tables(length, sky_count)
    mix = tile_table(width).reshape(-1)
    chunks = next(n for n in (4, 2, 1) if groups % n == 0)
    peers = (sky_count, -(-(groups // chunks * part + 2) // SUB) * SUB, rows)
    scaled = (sky_count, groups // chunks * part + SUB, rows)
    operands = (density, refine[0], weight_low, weight_high, table, forward, twist, mix)
    dma = pltpu.SemaphoreType.DMA
    f32, i32 = jnp.float32, jnp.int32
    planes = pl.pallas_call(
        functools.partial(lens_kernel, length, los_count, sky_count, groups, chunks),
        out_shape=(jax.ShapeDtypeStruct((rows, width // los_count), f32),) * 2,
        in_specs=[HBM] * 8,
        out_specs=(VMEM, VMEM),
        scratch_shapes=[
            pltpu.VMEM((slab, rows, width), density.dtype),
            pltpu.VMEM((slab, tiles, rows + 2 * SUB, LANES), f32),
            pltpu.VMEM((rows, width), density.dtype),
            pltpu.VMEM((rows, width), density.dtype),
            pltpu.VMEM((tiles, refine.shape[1], LANES), f32),
            pltpu.VMEM((4, tiles, rows, LANES), f32),
            pltpu.VMEM((tiles, rows, LANES), f32),
            pltpu.VMEM((tiles, rows + 2 * SUB, LANES), f32),
            pltpu.VMEM((tiles, rows + 2 * SUB, LANES), f32),
            pltpu.VMEM((los_count, groups, 2, rows, LANES), f32),
            pltpu.VMEM((los_count - 1, groups, rows + SUB, LANES), i32),
            pltpu.VMEM((los_count - 1, groups, rows + SUB, LANES), i32),
            pltpu.VMEM(table.shape, f32),
            pltpu.VMEM(forward.shape, f32),
            pltpu.VMEM(twist.shape, f32),
            pltpu.VMEM(refine.shape[1:], i32),
            pltpu.SMEM((slab,), f32),
            pltpu.SMEM((slab,), f32),
            pltpu.SMEM(mix.shape, f32),
            pltpu.VMEM((groups, 2, LANES, rows), f32),
            pltpu.VMEM((chunks,) + peers, i32),
            pltpu.VMEM((chunks,) + peers, i32),
            pltpu.VMEM((2, chunks) + peers, i32),
            pltpu.VMEM((2, chunks) + peers, i32),
            pltpu.VMEM((los_count - 1, 2, chunks) + peers, i32),
            pltpu.VMEM((chunks, 2) + scaled, f32),
            dma((7,)),
            dma((rows // 16,)),
            dma((2, 4)),
            dma((2, 4)),
            dma((6,)),
            dma((6,)),
            dma((los_count, groups)),
            dma((los_count, groups)),
            dma((chunks,)),
            dma((chunks,)),
            dma((2, chunks)),
            dma((2, chunks)),
            dma((2, chunks, los_count)),
            dma((2, chunks, los_count)),
        ],
        compiler_params=pltpu.CompilerParams(
            vmem_limit_bytes=48 * 1024 * 1024, collective_id=0, has_side_effects=True
        ),
    )(*[pltpu.with_memory_space_constraint(x, pltpu.HBM) for x in operands])
    return pl.pallas_call(
        emit_kernel,
        out_shape=tuple(jax.ShapeDtypeStruct(plane.shape, f32) for plane in planes),
        in_specs=[ANY, ANY],
        out_specs=(HBM, HBM),
        scratch_shapes=[dma((2,))],
        compiler_params=pltpu.CompilerParams(vmem_limit_bytes=1024 * 1024),
    )(*planes)


def solution(mesh):
    placed = (P("los", "sky", None), P("los", "sky", None), P("los"), P("los"))
    return jax.shard_map(
        body,
        mesh=mesh,
        in_specs=placed,
        out_specs=(P("sky", "los"), P("sky", "los")),
        check_vma=False,
    )
```
